32 devices in a mesh: feed: 4 (over y, core), tm: 8 (over z, x).
Axes of the slice: x: 2, y: 2, z: 4, core: 2. Of those that a mesh axis runs over, the one named last changes fastest.
Arguments:
- tod: bfloat16 [8192, 50, 256], P(('feed', 'tm')), may hold values from -6 to 6
- pixels: int32 [8192, 50], P(('feed', 'tm')), may hold values from 0 to 31
- block_slots: int32 [8192], P(('feed', 'tm')), may hold values from 0 to 7, as said below
- tile_lists: int32 [32, 8, 1], P(('feed', 'tm')), may hold values from -1 to 63, as said below
- tile_place: int32 [64], replicated, may hold values from 0 to 63, as said below
- prior: float32 [256], replicated, may hold values from 0.5 to 4
Outputs:
- drift_levels: float32 [8192, 256], P(('feed', 'tm'))
- leftover_error: float32 [8192, 256], P(('feed', 'tm'))
- destriped_result_map: float32 [64, 32, 256], P('tm', None, 'feed')
The draws below stay inside these ranges and needn't reach their ends.
Inputs may be any that keep to these rules, and one draw needn't show every extreme that they name: tile_lists[g, o, s] is -1 or a tile whose tile_place // 8 equals o; the live entries of one device are distinct; entries 0 and 7 of each device's flattened list are live; some tiles are named by no list. block_slots[b] names a live entry of the flattened list of the device that holds baseline b. tile_place is a permutation of the tiles; place p is stored by tm index p // 8 in its row p % 8.
All inputs are finite; a program needn't handle non-finite values.
Results may differ from the reference program's by a relative error of at most 0.0013.
Values sent between devices are 32-bit elements; how exact they have to be, the bound alone decides.
No kernel may reach another device: no remote copies, remote signals or barrier semaphores. Data moves between devices by JAX's collectives and lax.ppermute only.
A program may use at most 64 MiB of HBM per device.

```python
import math
import jax
import jax.numpy as jnp

CHANNEL_NUMBER = 256
BASE = 50
CELLS_IN_PATCH = 32
TILES_DEV = 8
SLOTS = 1
ITERS = 2
BLOCKS_DEV = 256
NBLOCKS = 8192
PATCH_NUMBER = 64
N_FEED = 4
N_TM = 8


def layout(key):
    tm_count = N_TM
    dev_count = N_FEED * N_TM
    slot_count = N_TM * SLOTS
    tile_total = TILES_DEV * N_TM
    place = jax.random.permutation(jax.random.fold_in(key, 11), tile_total).astype(jnp.int32)
    owned = jnp.argsort(place).astype(jnp.int32).reshape(tm_count, TILES_DEV)
    excluded = jax.random.randint(jax.random.fold_in(key, 15), (), 0, tile_total - 1)
    ex_place = place[excluded]
    ex_owner = ex_place // TILES_DEV
    ex_row = ex_place % TILES_DEV
    start_all = jax.random.randint(jax.random.fold_in(key, 12), (dev_count, tm_count, 1), 0, TILES_DEV)
    start_cut = jax.random.randint(jax.random.fold_in(key, 16), (dev_count, tm_count, 1), 0, TILES_DEV - 1)
    offsets = jnp.arange(SLOTS, dtype=jnp.int32)[None, None, :]
    owners = jnp.broadcast_to(jnp.arange(tm_count, dtype=jnp.int32)[None, :, None], (dev_count, tm_count, SLOTS))
    local_all = (start_all + offsets) % TILES_DEV
    local_cut = (start_cut + offsets) % (TILES_DEV - 1)
    local_cut = local_cut + (local_cut >= ex_row).astype(jnp.int32)
    local = jnp.where(owners == ex_owner, local_cut, local_all)
    tiles = owned[owners, local]
    last_owner = place[tile_total - 1] // TILES_DEV
    tiles = tiles.at[0, last_owner, 0].set(tile_total - 1)
    tiles = tiles.reshape(dev_count, slot_count)
    live = jax.random.randint(jax.random.fold_in(key, 13), (dev_count, slot_count), 0, 8) < 7
    live = live.at[:, 0].set(True).at[:, slot_count - 1].set(True)
    live = live.at[0, last_owner * SLOTS].set(True)
    lists = jnp.where(live, tiles, -1).astype(jnp.int32).reshape(dev_count, tm_count, SLOTS)
    counts = jnp.cumsum(live.astype(jnp.int32), axis=1)
    total = counts[:, -1:]
    raw = jax.random.randint(jax.random.fold_in(key, 14), (dev_count, BLOCKS_DEV), 0, 1 << 20)
    wanted = raw % total
    slots = jnp.sum((counts[:, None, :] <= wanted[:, :, None]).astype(jnp.int32), axis=2)
    slots = slots.at[:, 0].set(slot_count - 1).at[:, 1].set(0)
    return (place, lists, slots.reshape(dev_count * BLOCKS_DEV).astype(jnp.int32))


def draw_tile_place(key, part):
    return layout(key)[0]


def draw_tile_lists(key, part):
    return layout(key)[1]


def draw_block_slots(key, part):
    return layout(key)[2]


def plant(values, rng, least, top_value):
    spot = [jax.random.randint(jax.random.fold_in(rng, axis), (), 0, length) for axis, length in enumerate(values.shape)]
    main_axis = values.shape.index(max(values.shape))
    next_to = spot[:main_axis] + [(spot[main_axis] + 1) % values.shape[main_axis]] + spot[main_axis + 1:]
    return values.at[tuple(spot)].set(least).at[tuple(next_to)].set(top_value)


def level_of(rng, shape, pieces, smallest, high):
    gain, own = 1.0, jax.random.fold_in(rng, 6)
    for axis_at, blocks in pieces:
        steps = jnp.exp(jax.random.uniform(jax.random.fold_in(own, axis_at), (blocks,), jnp.float32, smallest / len(pieces), high / len(pieces)))
        gain = gain * jnp.repeat(steps, shape[axis_at] // blocks).reshape([-1 if axis == axis_at else 1 for axis in range(len(shape))])
    return gain


def centred(own_key, extent, deviation, limit, pieces=(), kind=jnp.bfloat16):
    level = level_of(own_key, extent, pieces, -0.22, 0.18) if pieces else 1.0
    array = jax.random.normal(own_key, extent, jnp.float32) * deviation * level
    return jnp.minimum(jnp.maximum(array, -limit), limit).astype(kind)


def setup_inputs(seed: int = 0) -> dict:
    keys = jax.random.split(jax.random.key(seed), 7)
    return {
        "tod": centred(keys[0], (NBLOCKS, BASE, CHANNEL_NUMBER), 1.0, 6.0, ((0, 32),)),
        "pixels": plant(jax.random.randint(keys[1], (NBLOCKS, BASE), 0, CELLS_IN_PATCH), jax.random.fold_in(keys[1], 1), 0, CELLS_IN_PATCH - 1).astype(jnp.int32),
        "block_slots": draw_block_slots(jax.random.fold_in(keys[6], 71), 0),
        "tile_lists": draw_tile_lists(jax.random.fold_in(keys[6], 71), 0),
        "tile_place": draw_tile_place(jax.random.fold_in(keys[6], 71), 0),
        "prior": jnp.clip(jnp.exp(jax.random.uniform(keys[5], (CHANNEL_NUMBER,), jnp.float32, math.log(0.5), math.log(4.0))), 0.5, 4.0),
    }


def reference(tod, pixels, block_slots, tile_lists, tile_place, prior):
    dev_count = N_FEED * N_TM
    slot_count = N_TM * SLOTS
    pix_total = PATCH_NUMBER * CELLS_IN_PATCH
    flat_lists = tile_lists.reshape(dev_count, slot_count)
    holder = jnp.arange(NBLOCKS, dtype=jnp.int32) // BLOCKS_DEV
    block_tile = flat_lists[holder, block_slots]
    gpix = (block_tile[:, None] * CELLS_IN_PATCH + pixels).reshape(-1).astype(jnp.int32)
    hits = jax.ops.segment_sum(jnp.ones((NBLOCKS * BASE,), jnp.float32), gpix, pix_total)
    inverse = 1.0 / jnp.maximum(hits, 1.0)

    def averaged_map_estimate(stream):
        summed = jax.ops.segment_sum(stream.reshape(-1, CHANNEL_NUMBER), gpix, pix_total)
        return summed * inverse[:, None]

    def project(stream):
        sky_now = averaged_map_estimate(stream)
        mapped = sky_now[gpix].reshape(stream.shape)
        return jnp.sum(stream - mapped, axis=1)

    def operate(values):
        stream = jnp.broadcast_to(values[:, None, :], (NBLOCKS, BASE, CHANNEL_NUMBER))
        return project(stream) + prior[None, :] * values

    detector_readings = tod.astype(jnp.float32)
    system_target = project(detector_readings)
    drift_levels = jnp.zeros_like(system_target)
    leftover_error = system_target
    descent_direction = system_target
    norm_now = jnp.sum(leftover_error * leftover_error)
    for number in range(ITERS):
        image = operate(descent_direction)
        update_factor = norm_now / jnp.sum(descent_direction * image)
        drift_levels = drift_levels + update_factor * descent_direction
        leftover_error = leftover_error - update_factor * image
        norm_next = jnp.sum(leftover_error * leftover_error)
        descent_direction = leftover_error + (norm_next / norm_now) * descent_direction
        norm_now = norm_next
    converged_drift_levels = averaged_map_estimate(detector_readings - drift_levels[:, None, :]).reshape(PATCH_NUMBER, CELLS_IN_PATCH, CHANNEL_NUMBER)
    destriped_result_map = jnp.zeros_like(converged_drift_levels).at[tile_place].set(converged_drift_levels)
    return drift_levels, leftover_error, destriped_result_map
```

```python
import jax
import jax.numpy as jnp
from jax import lax
from jax.experimental import pallas as pl
from jax.experimental.pallas import tpu as pltpu
from jax.sharding import PartitionSpec as P

CELLS = 32
EXACT = lax.Precision.HIGHEST
f32 = jnp.float32
bf16 = jnp.bfloat16


def split3(value):
    high = value.astype(bf16)
    rest = value - high.astype(f32)
    mid = rest.astype(bf16)
    low = (rest - mid.astype(f32)).astype(bf16)
    return high, mid, low


def counted(counts, value):
    out = None
    for part in split3(value):
        term = jnp.dot(counts, part, preferred_element_type=f32)
        out = term if out is None else out + term
    return out


def shift_of(prior):
    return jnp.sum(prior, axis=1, keepdims=True) * (1.0 / prior.shape[1])


def bin_kernel(
    list_ref, place_ref, slot_ref, pix_ref, tod_ref,
    pay_ref, sums_ref, w_ref, power_ref,
    t_acc, s_acc, wt_acc, g_scr, v_scr,
    *, slots, feeds, rows_owned, step_samples,
):
    step = pl.program_id(0)
    blocks = slot_ref.shape[1]
    cells = slots * CELLS
    lanes = pay_ref.shape[2]
    width = lanes // 2
    base = slot_ref[...] * CELLS
    row_id = lax.broadcasted_iota(jnp.int32, (cells, blocks), 0)
    hots = []
    count = None
    total = None
    for j in range(step_samples):
        cell = base + pix_ref[pl.ds(step * step_samples + j, 1), :]
        hot = (row_id == cell).astype(f32)
        count = hot if count is None else count + hot
        hots.append(hot.astype(bf16))
        now = tod_ref[j].astype(f32)
        total = now if total is None else total + now
    hot_all = jnp.concatenate(hots, axis=1)
    tod_all = tod_ref[...].reshape(step_samples * blocks, tod_ref.shape[2])
    binned = jnp.dot(hot_all, tod_all, preferred_element_type=f32)

    @pl.when(step == 0)
    def _():
        t_acc[...] = binned
        s_acc[...] = total
        wt_acc[...] = count

    @pl.when(step > 0)
    def _():
        t_acc[...] += binned
        s_acc[...] += total
        wt_acc[...] += count

    @pl.when(step == pl.num_programs(0) - 1)
    def _():
        sums = s_acc[...]
        wt = wt_acc[...].astype(bf16)
        sums_ref[...] = sums
        w_ref[...] = wt_acc[...].T.astype(bf16)
        power_ref[...] = jnp.sum(sums * sums, axis=0, keepdims=True)
        v_scr[...] = counted(wt, sums)
        g_scr[...] = lax.dot_general(wt, wt, (((1,), (1,)), ((), ())), preferred_element_type=f32)
        nb = lanes // CELLS
        rb = CELLS // nb
        sub = lax.broadcasted_iota(jnp.int32, (rb, lanes), 0)
        lane = lax.broadcasted_iota(jnp.int32, (rb, lanes), 1)
        mark = (sub == rb - 1) & (lane == (nb - 1) * CELLS)
        for k in range(slots):
            q0 = k * CELLS
            pack = jnp.concatenate(
                [g_scr[q0 + rb * i:q0 + rb * (i + 1), q0:q0 + CELLS] for i in range(nb)], axis=1
            )
            tile = list_ref[k]
            row = jnp.where(tile >= 0, lax.rem(place_ref[jnp.maximum(tile, 0)], rows_owned), -1)
            pack = jnp.where(mark, row.astype(f32), pack)
            for f in range(feeds):
                d = f * slots + k
                pay_ref[d, 0:CELLS, :] = jnp.concatenate(
                    [
                        t_acc[q0:q0 + CELLS, f * width:(f + 1) * width],
                        v_scr[q0:q0 + CELLS, f * width:(f + 1) * width],
                    ],
                    axis=1,
                )
                pay_ref[d, CELLS:CELLS + rb, :] = pack


def expand(gram_ref, k, pack, nb, rb):
    for i in range(nb):
        gram_ref[k * CELLS + rb * i:k * CELLS + rb * (i + 1), k * CELLS:(k + 1) * CELLS] = (
            pack[:, i * CELLS:(i + 1) * CELLS]
        )


def owner_kernel(
    feed_ref, recv_ref, prior_ref, power_ref,
    pay_ref, map_ref,
    acc_ref, gram_ref, pair_ref,
    *, feeds, rows_owned, samples,
):
    sources, rows, lanes = recv_ref.shape
    width = lanes // 2
    nb = lanes // CELLS
    rb = CELLS // nb
    tiles = rows // 8
    mark_row = CELLS + rb - 1
    mark_lane = (nb - 1) * CELLS

    def gather(d, accs):
        index = jnp.broadcast_to(recv_ref[d, mark_row:mark_row + 1, mark_lane:mark_lane + 1], (8, lanes))
        values = [recv_ref[d, 8 * j:8 * j + 8, :] for j in range(tiles)]
        out = []
        for r in range(rows_owned):
            hit = index == float(r)
            for j in range(tiles):
                out.append(accs[r * tiles + j] + jnp.where(hit, values[j], 0.0))
        return tuple(out)

    zero = jnp.zeros((8, lanes), f32)
    accs = lax.fori_loop(0, sources, gather, (zero,) * (rows_owned * tiles), unroll=4)
    for r in range(rows_owned):
        for j in range(tiles):
            acc_ref[r, 8 * j:8 * j + 8, :] = accs[r * tiles + j]
    gram_ref[...] = jnp.zeros(gram_ref.shape, f32)
    sub = lax.broadcasted_iota(jnp.int32, (rb, lanes), 0)
    lane = lax.broadcasted_iota(jnp.int32, (rb, lanes), 1)
    mark = (sub == rb - 1) & (lane == mark_lane)
    packs = []
    for r in range(rows_owned):
        pack = acc_ref[r, CELLS:CELLS + rb, :]
        pack = jnp.where(mark, pack[0:1, CELLS - 1:CELLS], pack)
        packs.append(pack)
        expand(gram_ref, r, pack, nb, rb)
    gram = gram_ref[...]
    hits = jnp.sum(gram, axis=1, keepdims=True) / float(samples)
    inverse = 1.0 / jnp.maximum(hits, 1.0)
    both = jnp.concatenate([acc_ref[r, 0:CELLS, :] for r in range(rows_owned)], axis=0)
    t_sum = both[:, 0:width]
    v_sum = both[:, width:lanes]
    prior = prior_ref[...]
    offset = prior - shift_of(prior)
    feed = feed_ref[0]
    mine = offset[:, 0:width]
    for f in range(1, feeds):
        mine = jnp.where(feed == f, offset[:, f * width:(f + 1) * width], mine)
    y0 = t_sum * inverse
    u0 = v_sum - jnp.dot(gram, y0, precision=EXACT, preferred_element_type=f32)
    y1 = u0 * inverse
    uz = mine * u0 - jnp.dot(gram, y1, precision=EXACT, preferred_element_type=f32)
    y2 = uz * inverse
    map_ref[0] = y0
    map_ref[1] = y1
    map_ref[2] = y2
    rr = -jnp.sum(y0 * (v_sum + u0), axis=0, keepdims=True)
    cross = jnp.sum(u0 * y1, axis=0, keepdims=True)
    zz = mine * mine * rr - jnp.sum(y1 * (mine * u0 + uz), axis=0, keepdims=True)
    zw = mine * zz - jnp.sum(uz * y2, axis=0, keepdims=True)
    rz = mine * rr - cross
    power = power_ref[...]
    parts = []
    for own in (rr, rz, zz, zw):
        for f in range(feeds):
            own = own + power[:, f * width:(f + 1) * width]
        parts.append(own)
        power = power * offset
    scal0 = jnp.concatenate(parts[0:2], axis=1)
    scal1 = jnp.concatenate(parts[2:4], axis=1)
    pair_ref[...] = jnp.concatenate([y0, y1], axis=1)
    share = rb // feeds
    fill = jnp.zeros((rows - CELLS - share - 2, lanes), f32)
    tails = []
    for r in range(rows_owned):
        quarter = packs[r][0:share]
        for f in range(1, feeds):
            quarter = jnp.where(feed == f, packs[r][f * share:(f + 1) * share], quarter)
        tails.append(jnp.concatenate([quarter, scal0, scal1, fill], axis=0))

    def scatter(d, carry):
        index = jnp.broadcast_to(recv_ref[d, mark_row:mark_row + 1, mark_lane:mark_lane + 1], (8, lanes))
        hits_r = [index == float(r) for r in range(rows_owned)]
        for j in range(CELLS // 8):
            v = jnp.zeros((8, lanes), f32)
            for r in range(rows_owned):
                v = jnp.where(hits_r[r], pair_ref[r * CELLS + 8 * j:r * CELLS + 8 * j + 8, :], v)
            pay_ref[d, 8 * j:8 * j + 8, :] = v
        for j in range((rows - CELLS) // 8):
            v = tails[0][8 * j:8 * j + 8]
            for r in range(1, rows_owned):
                v = jnp.where(hits_r[r], tails[r][8 * j:8 * j + 8], v)
            pay_ref[d, CELLS + 8 * j:CELLS + 8 * j + 8, :] = v
        return carry

    lax.fori_loop(0, sources, scatter, 0, unroll=4)


def final_kernel(
    recv_ref, prior_ref, sums_ref, w_ref, maps_ref, feed_ref,
    x_ref, r_ref, out_ref,
    gram_ref, y0_ref, y1_ref,
    *, slots, feeds, samples,
):
    sources, rows, lanes = recv_ref.shape
    width = lanes // 2
    nb = lanes // CELLS
    rb = CELLS // nb
    share = rb // feeds
    prior = prior_ref[...]
    mean = shift_of(prior)
    offset = prior - mean
    sigma = mean + float(samples)
    scal = jnp.sum(recv_ref[:, CELLS + share:CELLS + share + 2, :], axis=0)
    rr0 = jnp.sum(scal[0:1, 0:width], axis=1, keepdims=True)
    rz = jnp.sum(scal[0:1, width:lanes], axis=1, keepdims=True)
    zz = jnp.sum(scal[1:2, 0:width], axis=1, keepdims=True)
    zw = jnp.sum(scal[1:2, width:lanes], axis=1, keepdims=True)
    gamma = rz / rr0
    alpha0 = 1.0 / (sigma + gamma)
    ee = zz - gamma * rz
    rr1 = alpha0 * alpha0 * ee
    beta = rr1 / rr0
    e_a_e = sigma * ee + (zw - 2.0 * gamma * zz + gamma * gamma * rz)
    alpha1 = rr1 / (alpha0 * alpha0 * e_a_e - rr1 * beta / alpha0)
    lead = alpha0 * gamma + beta
    slack = 1.0 - alpha1 * sigma
    x_r = alpha0 + alpha1 * lead
    x_z = -alpha0 * alpha1
    r_r = alpha0 * gamma * slack - alpha1 * sigma * beta
    r_z = -alpha0 * slack - alpha1 * lead
    r_w = alpha0 * alpha1
    gram_ref[...] = jnp.zeros(gram_ref.shape, f32)
    for k in range(slots):
        pack = jnp.concatenate(
            [recv_ref[f * slots + k, CELLS:CELLS + share, :] for f in range(feeds)], axis=0
        )
        expand(gram_ref, k, pack, nb, rb)
        y0_ref[k * CELLS:(k + 1) * CELLS, :] = jnp.concatenate(
            [recv_ref[f * slots + k, 0:CELLS, 0:width] for f in range(feeds)], axis=1
        )
        y1_ref[k * CELLS:(k + 1) * CELLS, :] = jnp.concatenate(
            [recv_ref[f * slots + k, 0:CELLS, width:lanes] for f in range(feeds)], axis=1
        )
    gram = gram_ref[...]
    hits = jnp.sum(gram, axis=1, keepdims=True) / float(samples)
    inverse = 1.0 / jnp.maximum(hits, 1.0)
    y0 = y0_ref[...]
    y1 = y1_ref[...]
    y2 = offset * y1 - inverse * jnp.dot(gram, y1, precision=EXACT, preferred_element_type=f32)
    sums = sums_ref[...]
    w = w_ref[...]
    lead_x = x_r + x_z * offset
    x_ref[...] = lead_x * sums - counted(w, lead_x * y0 + x_z * y1)
    second = r_z + r_w * offset
    lead_r = r_r + second * offset
    r_ref[...] = lead_r * sums - counted(w, lead_r * y0 + second * y1 + r_w * y2)
    out_ref[...] = maps_ref[0] - x_r * maps_ref[1] - x_z * maps_ref[2]


def local(tod, pixels, block_slots, tile_lists, tile_place, prior):
    axes = ("feed", "tm")
    feeds = lax.axis_size("feed")
    owners = lax.axis_size("tm")
    slots = tile_lists.shape[1] * tile_lists.shape[2]
    assert slots == owners
    rows_owned = tile_place.shape[0] // owners
    blocks, samples, channels = tod.shape
    cells = slots * CELLS
    width = channels // feeds
    lanes = 2 * width
    gram_rows = CELLS * CELLS // lanes
    rows = CELLS + gram_rows
    devices = feeds * owners
    step_samples = max(n for n in range(1, 11) if samples % n == 0)
    smem = pl.BlockSpec(memory_space=pltpu.SMEM)
    vmem = pl.BlockSpec(memory_space=pltpu.VMEM)

    def whole(*shape):
        return pl.BlockSpec(shape, lambda i: (0,) * len(shape))

    payload, sums, weights, power = pl.pallas_call(
        lambda *refs: bin_kernel(
            *refs, slots=slots, feeds=feeds, rows_owned=rows_owned, step_samples=step_samples
        ),
        grid=(samples // step_samples,),
        in_specs=[
            smem,
            smem,
            whole(1, blocks),
            whole(samples, blocks),
            pl.BlockSpec((step_samples, blocks, channels), lambda i: (i, 0, 0)),
        ],
        out_specs=[
            whole(devices, rows, lanes),
            whole(blocks, channels),
            whole(blocks, cells),
            whole(1, channels),
        ],
        out_shape=[
            jax.ShapeDtypeStruct((devices, rows, lanes), f32),
            jax.ShapeDtypeStruct((blocks, channels), f32),
            jax.ShapeDtypeStruct((blocks, cells), bf16),
            jax.ShapeDtypeStruct((1, channels), f32),
        ],
        scratch_shapes=[
            pltpu.VMEM((cells, channels), f32),
            pltpu.VMEM((blocks, channels), f32),
            pltpu.VMEM((cells, blocks), f32),
            pltpu.VMEM((cells, cells), f32),
            pltpu.VMEM((cells, channels), f32),
        ],
        name="bin_samples",
    )(
        tile_lists.reshape(slots),
        tile_place,
        block_slots.reshape(1, blocks),
        pixels.T,
        tod.transpose(1, 0, 2),
    )
    received = lax.all_to_all(payload, axes, split_axis=0, concat_axis=0, tiled=True)
    feed = lax.axis_index("feed").astype(jnp.int32).reshape(1)
    prior_row = prior.reshape(1, channels)
    owned_cells = rows_owned * CELLS
    answer, maps = pl.pallas_call(
        lambda *refs: owner_kernel(*refs, feeds=feeds, rows_owned=rows_owned, samples=samples),
        in_specs=[smem, vmem, vmem, vmem],
        out_specs=[vmem, vmem],
        out_shape=[
            jax.ShapeDtypeStruct((devices, rows, lanes), f32),
            jax.ShapeDtypeStruct((3, owned_cells, width), f32),
        ],
        scratch_shapes=[
            pltpu.VMEM((rows_owned, rows, lanes), f32),
            pltpu.VMEM((owned_cells, owned_cells), f32),
            pltpu.VMEM((owned_cells, lanes), f32),
        ],
        name="solve_tiles",
    )(feed, received, prior_row, power)
    returned = lax.all_to_all(answer, axes, split_axis=0, concat_axis=0, tiled=True)
    drift, leftover, sky = pl.pallas_call(
        lambda *refs: final_kernel(*refs, slots=slots, feeds=feeds, samples=samples),
        in_specs=[vmem, vmem, vmem, vmem, vmem, smem],
        out_specs=[vmem, vmem, vmem],
        out_shape=[
            jax.ShapeDtypeStruct((blocks, channels), f32),
            jax.ShapeDtypeStruct((blocks, channels), f32),
            jax.ShapeDtypeStruct((owned_cells, width), f32),
        ],
        scratch_shapes=[
            pltpu.VMEM((cells, cells), f32),
            pltpu.VMEM((cells, channels), f32),
            pltpu.VMEM((cells, channels), f32),
        ],
        name="finish",
    )(returned, prior_row, sums, weights, maps, feed)
    return drift, leftover, sky.reshape(rows_owned, CELLS, width)


def solution(mesh):
    return jax.shard_map(
        local,
        mesh=mesh,
        in_specs=(
            P(("feed", "tm"), None, None),
            P(("feed", "tm"), None),
            P(("feed", "tm")),
            P(("feed", "tm"), None, None),
            P(),
            P(),
        ),
        out_specs=(P(("feed", "tm"), None), P(("feed", "tm"), None), P("tm", None, "feed")),
        check_vma=False,
    )
```

```python
import jax
import jax.numpy as jnp
from jax import lax
from jax.experimental import pallas as pl
from jax.experimental.pallas import tpu as pltpu
from jax.sharding import PartitionSpec as P

CELLS = 32
EXACT = lax.Precision.HIGHEST
f32 = jnp.float32
bf16 = jnp.bfloat16


def split3(value):
    high = value.astype(bf16)
    rest = value - high.astype(f32)
    mid = rest.astype(bf16)
    low = (rest - mid.astype(f32)).astype(bf16)
    return high, mid, low


def counted(counts, value):
    out = None
    for part in split3(value):
        term = jnp.dot(counts, part, preferred_element_type=f32)
        out = term if out is None else out + term
    return out


def near(value, small):
    return pltpu.with_memory_space_constraint(value, pltpu.VMEM) if small else value


def shift_of(prior):
    return jnp.sum(prior, axis=1, keepdims=True) * (1.0 / prior.shape[1])


def bin_kernel(
    feed_ref, list_ref, place_ref, slot_ref, pix_ref, tod_ref,
    pay_ref, sums_ref, w_ref, power_ref,
    tod_buf, hot_ref, t_acc, wt_acc, sems,
    *, slots, feeds, rows_owned, chunk,
):
    samples, blocks, channels = tod_ref.shape
    cells = slots * CELLS
    lanes = pay_ref.shape[2]
    width = lanes // 2
    chunks = samples // chunk
    kind = bf16 if cells <= 256 else f32
    copies = [
        pltpu.make_async_copy(
            tod_ref.at[pl.ds(i * chunk, chunk)], tod_buf.at[pl.ds(i * chunk, chunk)], sems.at[i]
        )
        for i in range(chunks)
    ]
    for copy in copies:
        copy.start()
    base = slot_ref[...] * CELLS
    one = jnp.ones((), kind)
    nil = jnp.zeros((), kind)

    def mark_hot(i):
        spread = [
            jnp.broadcast_to((base + pix_ref[s:s + 1, :]).astype(f32).astype(kind), (16, blocks))
            for s in range(i * chunk, (i + 1) * chunk)
        ]
        for q in range(0, cells, 16):
            row = (lax.broadcasted_iota(jnp.int32, (16, blocks), 0) + q).astype(f32).astype(kind)
            count = None
            for j in range(chunk):
                s = i * chunk + j
                hot = jnp.where(row == spread[j], one, nil)
                hot_ref[q:q + 16, s * blocks:(s + 1) * blocks] = hot.astype(bf16)
                count = hot if count is None else count + hot
            if i > 0:
                count = count + wt_acc[q:q + 16, :]
            wt_acc[q:q + 16, :] = count

    def pack_counts():
        wt = wt_acc[...].astype(bf16)
        w_ref[...] = wt.T
        nb = lanes // CELLS
        rb = CELLS // nb
        every = wt_acc[0:CELLS, :].astype(f32)
        for k in range(1, slots):
            every = every + wt_acc[k * CELLS:(k + 1) * CELLS, :].astype(f32)
        every = jnp.concatenate([every.astype(bf16)] * nb, axis=0)
        gram = lax.dot_general(wt, every, (((1,), (1,)), ((), ())), preferred_element_type=f32)
        sub = lax.broadcasted_iota(jnp.int32, (rb, lanes), 0)
        lane = lax.broadcasted_iota(jnp.int32, (rb, lanes), 1)
        mark = (sub == rb - 1) & (lane == (nb - 1) * CELLS)
        for k in range(slots):
            pack = gram[k * CELLS:k * CELLS + rb]
            for i in range(1, nb):
                piece = gram[k * CELLS + rb * i:k * CELLS + rb * (i + 1)]
                pack = jnp.where(lane >= i * CELLS, piece, pack)
            tile = list_ref[k]
            row = jnp.where(tile >= 0, lax.rem(place_ref[jnp.maximum(tile, 0)], rows_owned), -1)
            pack = jnp.where(mark, row.astype(f32), pack)
            for f in range(feeds):
                pay_ref[f * slots + k, CELLS:CELLS + rb, :] = pack

    mark_hot(0)
    for i in range(chunks):
        if i + 1 < chunks:
            mark_hot(i + 1)
        else:
            pack_counts()
        copies[i].wait()
        first = i * chunk
        now = tod_buf[first:first + chunk].reshape(chunk * blocks, channels)
        binned = jnp.dot(
            hot_ref[:, first * blocks:(first + chunk) * blocks], now, preferred_element_type=f32
        )
        t_acc[...] = binned if i == 0 else t_acc[...] + binned
        for b in range(0, blocks, 16):
            total = sums_ref[b:b + 16, :] if i else None
            for s in range(first, first + chunk):
                part = tod_buf[s, b:b + 16, :].astype(f32)
                total = part if total is None else total + part
            sums_ref[b:b + 16, :] = total

    sums = sums_ref[...]
    power_ref[...] = jnp.sum(sums * sums, axis=0, keepdims=True)
    cross = counted(wt_acc[...].astype(bf16), sums)
    for k in range(slots):
        q0 = k * CELLS
        for f in range(feeds):
            pay_ref[f * slots + k, 0:CELLS, :] = jnp.concatenate(
                [
                    t_acc[q0:q0 + CELLS, f * width:(f + 1) * width],
                    cross[q0:q0 + CELLS, f * width:(f + 1) * width],
                ],
                axis=1,
            )


def turn(value, shift):
    lanes = value.shape[1]
    shift = shift % lanes
    if shift == 0:
        return value
    if lanes % 128 == 0:
        return pltpu.roll(value, shift, 1)
    return jnp.concatenate([value[:, lanes - shift:], value[:, :lanes - shift]], axis=1)


def gram_blocks(packs):
    rb, lanes = packs[0].shape
    nb = lanes // CELLS
    lane = lax.broadcasted_iota(jnp.int32, (rb, lanes), 1)
    blocks = []
    for first in range(0, len(packs), nb):
        rows = []
        for j in range(nb):
            inside = (lane >= j * CELLS) & (lane < (j + 1) * CELLS)
            for i in range(nb):
                rows.append(jnp.where(inside, turn(packs[first + j], (j - i) * CELLS), 0.0))
        blocks.append(jnp.concatenate(rows, axis=0))
    return blocks


def stacked(block):
    return jnp.concatenate(split3(block), axis=0)


def gram_times(stack, value):
    n = stack.shape[1]
    total = None
    for j, part in enumerate(split3(value)):
        term = jnp.dot(stack[0:(3 - j) * n], part, preferred_element_type=f32)
        for i in range(3 - j):
            piece = term[i * n:(i + 1) * n]
            total = piece if total is None else total + piece
    return total


def gram_times_narrow(stack, value):
    n = stack.shape[1]
    w = value.shape[1]
    wide = jnp.dot(stack, jnp.concatenate(split3(value), axis=1), preferred_element_type=f32)
    wide = wide[2 * n:3 * n] + wide[n:2 * n] + wide[0:n]
    return wide[:, 2 * w:3 * w] + wide[:, w:2 * w] + wide[:, 0:w]


def owner_kernel(
    feed_ref, recv_ref, prior_ref, power_ref,
    pay_ref, map_ref,
    index_ref, acc_ref, pair_ref,
    *, feeds, rows_owned, samples, rows_out,
):
    sources, rows, lanes = recv_ref.shape
    width = lanes // 2
    nb = lanes // CELLS
    rb = CELLS // nb
    share = rb // feeds
    tiles = rows // 8
    mark_row = CELLS + rb - 1
    mark_lane = (nb - 1) * CELLS
    step = 8

    def spread(g, carry):
        for e in range(step):
            d = g * step + e
            index_ref[d] = jnp.broadcast_to(
                recv_ref[d, mark_row:mark_row + 1, mark_lane:mark_lane + 1], (8, lanes)
            )
        return carry

    lax.fori_loop(0, sources // step, spread, 0)
    for group in range(0, tiles, 2):
        members = range(group, min(group + 2, tiles))

        def gather(g, accs):
            accs = list(accs)
            for e in range(step):
                d = g * step + e
                index = index_ref[d]
                values = [recv_ref[d, 8 * j:8 * j + 8, :] for j in members]
                for r in range(rows_owned):
                    hit = index == float(r)
                    for n, value in enumerate(values):
                        at = r * len(values) + n
                        accs[at] = accs[at] + jnp.where(hit, value, 0.0)
            return tuple(accs)

        zero = jnp.zeros((8, lanes), f32)
        accs = lax.fori_loop(0, sources // step, gather, (zero,) * (rows_owned * len(members)))
        for r in range(rows_owned):
            for n, j in enumerate(members):
                acc_ref[r, 8 * j:8 * j + 8, :] = accs[r * len(members) + n]

    sub = lax.broadcasted_iota(jnp.int32, (rb, lanes), 0)
    lane = lax.broadcasted_iota(jnp.int32, (rb, lanes), 1)
    mark = (sub == rb - 1) & (lane == mark_lane)
    packs = []
    for r in range(rows_owned):
        pack = acc_ref[r, CELLS:CELLS + rb, :]
        packs.append(jnp.where(mark, pack[0:1, CELLS - 1:CELLS], pack))
    prior = prior_ref[...]
    offset = prior - shift_of(prior)
    feed = feed_ref[0]
    mine = offset[:, 0:width]
    for f in range(1, feeds):
        mine = jnp.where(feed == f, offset[:, f * width:(f + 1) * width], mine)
    rr = rz = zz = zw = None
    cross = half = last = None
    for g, block in enumerate(gram_blocks(packs)):
        stack = stacked(block)
        hits = jnp.sum(block, axis=1, keepdims=True) / float(samples)
        inverse = 1.0 / jnp.maximum(hits, 1.0)
        both = jnp.concatenate([acc_ref[r, 0:CELLS, :] for r in range(g * nb, (g + 1) * nb)], axis=0)
        v_sum = both[:, width:lanes]
        y0 = both[:, 0:width] * inverse
        u0 = v_sum - gram_times_narrow(stack, y0)
        y1 = u0 * inverse
        uz = mine * u0 - gram_times_narrow(stack, y1)
        y2 = uz * inverse
        q0 = g * nb * CELLS
        map_ref[0, q0:q0 + nb * CELLS, :] = y0
        map_ref[1, q0:q0 + nb * CELLS, :] = y1
        map_ref[2, q0:q0 + nb * CELLS, :] = y2
        pair_ref[q0:q0 + nb * CELLS, :] = jnp.concatenate([y0, y1], axis=1)
        terms = [
            jnp.sum(term, axis=0, keepdims=True)
            for term in (y0 * (v_sum + u0), u0 * y1, y1 * (mine * u0 + uz), uz * y2)
        ]
        if g == 0:
            rr, cross, half, last = terms
        else:
            rr, cross, half, last = rr + terms[0], cross + terms[1], half + terms[2], last + terms[3]
    rr = -rr
    rz = mine * rr - cross
    zz = mine * mine * rr - half
    zw = mine * zz - last
    power = power_ref[...]
    parts = []
    for own in (rr, rz, zz, zw):
        for f in range(feeds):
            own = own + power[:, f * width:(f + 1) * width]
        parts.append(own[:, 0:width // 2] + own[:, width // 2:width])
        power = power * offset
    scal = jnp.concatenate(parts, axis=1)
    tails = []
    for r in range(rows_owned):
        quarter = packs[r][0:share]
        for f in range(1, feeds):
            quarter = jnp.where(feed == f, packs[r][f * share:(f + 1) * share], quarter)
        tails.append(quarter)

    def scatter(d):
        index = index_ref[d]
        hits_r = [index == float(r) for r in range(rows_owned)]
        for j in range(CELLS // 8):
            v = pair_ref[8 * j:8 * j + 8, :]
            for r in range(1, rows_owned):
                v = jnp.where(hits_r[r], pair_ref[r * CELLS + 8 * j:r * CELLS + 8 * j + 8, :], v)
            pay_ref[pl.ds(d * rows_out + 8 * j, 8), :] = v
        v = tails[0]
        for r in range(1, rows_owned):
            v = jnp.where(hits_r[r][0:share], tails[r], v)
        if rows_out % 8:
            pay_ref[pl.ds(d * rows_out + CELLS, share + 1), :] = jnp.concatenate([v, scal], axis=0)
        else:
            fill = jnp.zeros((rows_out - CELLS - share - 1, lanes), f32)
            pay_ref[pl.ds(d * rows_out + CELLS, 8), :] = jnp.concatenate([v, scal, fill], axis=0)

    if rows_out % 8:
        for d in range(sources):
            scatter(d)
    else:
        lax.fori_loop(0, sources, lambda d, c: (scatter(d), c)[1], 0)


def final_kernel(
    recv_ref, prior_ref, sums_ref, w_ref, maps_ref,
    x_ref, r_ref, out_ref,
    y0_ref, y1_ref, y2_ref,
    *, slots, feeds, samples, share, rows_in,
):
    lanes = recv_ref.shape[1]
    sources = recv_ref.shape[0] // rows_in
    width = lanes // 2
    nb = lanes // CELLS
    prior = prior_ref[...]
    mean = shift_of(prior)
    offset = prior - mean
    sigma = mean + float(samples)
    scal = None
    for d in range(sources):
        now = recv_ref[d * rows_in + CELLS + share:d * rows_in + CELLS + share + 1, :]
        scal = now if scal is None else scal + now
    quarter = lanes // 4
    rr0, rz, zz, zw = [
        jnp.sum(scal[:, i * quarter:(i + 1) * quarter], axis=1, keepdims=True) for i in range(4)
    ]
    gamma = rz / rr0
    alpha0 = 1.0 / (sigma + gamma)
    ee = zz - gamma * rz
    rr1 = alpha0 * alpha0 * ee
    beta = rr1 / rr0
    e_a_e = sigma * ee + (zw - 2.0 * gamma * zz + gamma * gamma * rz)
    alpha1 = rr1 / (alpha0 * alpha0 * e_a_e - rr1 * beta / alpha0)
    lead = alpha0 * gamma + beta
    slack = 1.0 - alpha1 * sigma
    x_r = alpha0 + alpha1 * lead
    x_z = -alpha0 * alpha1
    r_r = alpha0 * gamma * slack - alpha1 * sigma * beta
    r_z = -alpha0 * slack - alpha1 * lead
    r_w = alpha0 * alpha1
    packs = []
    for k in range(slots):
        base = [(f * slots + k) * rows_in for f in range(feeds)]
        packs.append(
            jnp.concatenate([recv_ref[b + CELLS:b + CELLS + share, :] for b in base], axis=0)
        )
        y0_ref[k * CELLS:(k + 1) * CELLS, :] = jnp.concatenate(
            [recv_ref[b:b + CELLS, 0:width] for b in base], axis=1
        )
        y1_ref[k * CELLS:(k + 1) * CELLS, :] = jnp.concatenate(
            [recv_ref[b:b + CELLS, width:lanes] for b in base], axis=1
        )
    for g, block in enumerate(gram_blocks(packs)):
        stack = stacked(block)
        hits = jnp.sum(block, axis=1, keepdims=True) / float(samples)
        inverse = 1.0 / jnp.maximum(hits, 1.0)
        q0 = g * nb * CELLS
        y1 = y1_ref[q0:q0 + nb * CELLS, :]
        y2_ref[q0:q0 + nb * CELLS, :] = offset * y1 - inverse * gram_times(stack, y1)
    y0 = y0_ref[...]
    y1 = y1_ref[...]
    sums = sums_ref[...]
    w = w_ref[...]
    lead_x = x_r + x_z * offset
    x_ref[...] = lead_x * sums - counted(w, lead_x * y0 + x_z * y1)
    second = r_z + r_w * offset
    lead_r = r_r + second * offset
    r_ref[...] = lead_r * sums - counted(w, lead_r * y0 + second * y1 + r_w * y2_ref[...])
    out_ref[...] = maps_ref[0] - x_r * maps_ref[1] - x_z * maps_ref[2]


def local(tod, pixels, block_slots, tile_lists, tile_place, prior):
    axes = ("feed", "tm")
    feeds = lax.axis_size("feed")
    owners = lax.axis_size("tm")
    slots = tile_lists.shape[1] * tile_lists.shape[2]
    assert slots == owners
    rows_owned = tile_place.shape[0] // owners
    blocks, samples, channels = tod.shape
    cells = slots * CELLS
    width = channels // feeds
    lanes = 2 * width
    gram_rows = CELLS * CELLS // lanes
    rows = CELLS + gram_rows
    devices = feeds * owners
    chunk = max(n for n in range(1, 11) if samples % n == 0)
    small = devices * rows * lanes <= 1 << 18
    held = pltpu.VMEM if small else jax.ShapeDtypeStruct
    smem = pl.BlockSpec(memory_space=pltpu.SMEM)
    vmem = pl.BlockSpec(memory_space=pltpu.VMEM)

    feed = lax.axis_index("feed").astype(jnp.int32).reshape(1)
    payload, sums, weights, power = pl.pallas_call(
        lambda *refs: bin_kernel(*refs, slots=slots, feeds=feeds, rows_owned=rows_owned, chunk=chunk),
        in_specs=[smem, smem, smem, vmem, vmem, pl.BlockSpec(memory_space=pl.ANY)],
        out_specs=[vmem, vmem, vmem, vmem],
        out_shape=[
            held((devices, rows, lanes), f32),
            held((blocks, channels), f32),
            held((blocks, cells), bf16),
            held((1, channels), f32),
        ],
        scratch_shapes=[
            pltpu.VMEM((samples, blocks, channels), bf16),
            pltpu.VMEM((cells, samples * blocks), bf16),
            pltpu.VMEM((cells, channels), f32),
            pltpu.VMEM((cells, blocks), bf16 if cells <= 256 else f32),
            pltpu.SemaphoreType.DMA((samples // chunk,)),
        ],
        name="bin_samples",
    )(
        feed,
        tile_lists.reshape(slots),
        tile_place,
        block_slots.reshape(1, blocks),
        pixels.T,
        tod.transpose(1, 0, 2),
    )
    received = lax.all_to_all(payload, axes, split_axis=0, concat_axis=0, tiled=True)
    prior_row = prior.reshape(1, channels)
    owned_cells = rows_owned * CELLS
    share = gram_rows // feeds
    rows_back = CELLS + share + 1
    if not small:
        rows_back = -(-rows_back // 8) * 8
    answer, maps = pl.pallas_call(
        lambda *refs: owner_kernel(
            *refs, feeds=feeds, rows_owned=rows_owned, samples=samples, rows_out=rows_back
        ),
        in_specs=[smem, vmem, vmem, vmem],
        out_specs=[vmem, vmem],
        out_shape=[
            held((devices * rows_back, lanes), f32),
            held((3, owned_cells, width), f32),
        ],
        scratch_shapes=[
            pltpu.VMEM((devices, 8, lanes), f32),
            pltpu.VMEM((rows_owned, rows, lanes), f32),
            pltpu.VMEM((owned_cells, lanes), f32),
        ],
        name="solve_tiles",
    )(feed, near(received, small), prior_row, near(power, small))
    returned = lax.all_to_all(
        answer.reshape(devices, 1, rows_back * lanes), axes, split_axis=0, concat_axis=0, tiled=True
    ).reshape(devices * rows_back, lanes)
    drift, leftover, sky = pl.pallas_call(
        lambda *refs: final_kernel(
            *refs, slots=slots, feeds=feeds, samples=samples, share=share, rows_in=rows_back
        ),
        in_specs=[vmem, vmem, vmem, vmem, vmem],
        out_specs=[vmem, vmem, vmem],
        out_shape=[
            jax.ShapeDtypeStruct((blocks, channels), f32),
            jax.ShapeDtypeStruct((blocks, channels), f32),
            jax.ShapeDtypeStruct((owned_cells, width), f32),
        ],
        scratch_shapes=[
            pltpu.VMEM((cells, channels), f32),
            pltpu.VMEM((cells, channels), f32),
            pltpu.VMEM((cells, channels), f32),
        ],
        name="finish",
    )(near(returned, small), prior_row, near(sums, small), near(weights, small), near(maps, small))
    return drift, leftover, sky.reshape(rows_owned, CELLS, width)


def solution(mesh):
    return jax.shard_map(
        local,
        mesh=mesh,
        in_specs=(
            P(("feed", "tm"), None, None),
            P(("feed", "tm"), None),
            P(("feed", "tm")),
            P(("feed", "tm"), None, None),
            P(),
            P(),
        ),
        out_specs=(P(("feed", "tm"), None), P(("feed", "tm"), None), P("tm", None, "feed")),
        check_vma=False,
    )
```

```python
import functools

import jax
import jax.numpy as jnp
from jax import lax
from jax.experimental import pallas as pl
from jax.experimental.pallas import tpu as pltpu
from jax.sharding import PartitionSpec as P

CELLS = 32
EXACT = lax.Precision.HIGHEST
f32 = jnp.float32
bf16 = jnp.bfloat16


def split3(value):
    high = value.astype(bf16)
    rest = value - high.astype(f32)
    mid = rest.astype(bf16)
    low = (rest - mid.astype(f32)).astype(bf16)
    return high, mid, low


def counted(counts, value):
    out = None
    for part in split3(value):
        term = jnp.dot(counts, part, preferred_element_type=f32)
        out = term if out is None else out + term
    return out


def near(value, small):
    return pltpu.with_memory_space_constraint(value, pltpu.VMEM) if small else value


def shift_of(prior):
    return jnp.sum(prior, axis=1, keepdims=True) * (1.0 / prior.shape[1])


def pair_up(low, high):
    lane = lax.broadcasted_iota(jnp.int32, low.shape, 1)
    return jnp.where(lane < low.shape[1] // 2, low, high)


def bin_kernel(
    list_ref, place_ref, slot_ref, pix_ref, prior_ref, tod_ref,
    pay_ref, sums_ref, w_ref, power_ref, prior_out,
    tod_buf, wt_ref, t_ref, v_ref, g_ref, prior_sem, sems, *accs,
    slots, feeds, rows_owned, chunk,
):
    samples, blocks, channels = tod_ref.shape
    cells = slots * CELLS
    lanes = pay_ref.shape[2]
    width = lanes // 2
    nb = lanes // CELLS
    rb = CELLS // nb
    chunks = samples // chunk
    copies = [
        pltpu.make_async_copy(
            tod_ref.at[pl.ds(i * chunk, chunk)], tod_buf.at[pl.ds(i * chunk, chunk)], sems.at[i]
        )
        for i in range(chunks)
    ]
    for copy in copies:
        copy.start()
    extra = pltpu.make_async_copy(prior_ref, prior_out, prior_sem)
    extra.start()
    one = jnp.ones((), bf16)
    nil = jnp.zeros((), bf16)
    owner = jnp.broadcast_to(slot_ref[...], (16, blocks))
    row = lax.broadcasted_iota(jnp.int32, (16, blocks), 0)
    masks = [(owner == k).astype(f32).astype(bf16) for k in range(slots)]
    halves = [(row + q).astype(f32).astype(bf16) for q in range(0, CELLS, 16)]
    counts = [None] * len(halves)

    def hot_of(s):
        spread = jnp.broadcast_to(pix_ref[s:s + 1, :].astype(f32).astype(bf16), (16, blocks))
        hots = [jnp.where(half == spread, one, nil) for half in halves]
        for h, hot in enumerate(hots):
            counts[h] = hot if counts[h] is None else counts[h] + hot
        return jnp.concatenate([hot * masks[k] for k in range(slots) for hot in hots], axis=0)

    strips = range(0, blocks, 16)

    def add_strip(i, at):
        total = sums_ref[at:at + 16, :] if i else None
        for s in range(i * chunk, (i + 1) * chunk):
            part = tod_buf[s, at:at + 16, :].astype(f32)
            total = part if total is None else total + part
        sums_ref[at:at + 16, :] = total

    if accs:
        def push(s):
            pltpu.matmul_push_rhs(tod_buf[s], s // 2 % 2, s % 2)

        for i in range(chunks):
            copies[i].wait()
            first = i * chunk
            push(first)
            push(first + 1)
            done = 0
            for s in range(first, first + chunk):
                hot = hot_of(s)
                if s + 2 < first + chunk:
                    push(s + 2)
                pltpu.matmul_acc_lhs(accs[s % 2], hot, load_staged_rhs=s // 2 % 2)
                upto = len(strips) * (s + 1 - first) // chunk
                for at in strips[done:upto]:
                    add_strip(i, at)
                done = upto
    else:
        for i in range(chunks):
            copies[i].wait()
            first = i * chunk
            hot = jnp.concatenate([hot_of(s) for s in range(first, first + chunk)], axis=1)
            now = tod_buf[first:first + chunk].reshape(chunk * blocks, channels)
            binned = jnp.dot(hot, now, preferred_element_type=f32)
            t_ref[...] = binned if i == 0 else t_ref[...] + binned
            for at in strips:
                add_strip(i, at)

    hits = jnp.concatenate(counts, axis=0)
    wt = jnp.concatenate(
        [count * masks[k] for k in range(slots) for count in counts], axis=0
    )
    wt_ref[...] = wt
    w_ref[...] = wt.T
    sums = sums_ref[...]
    parts = split3(sums)
    if accs:
        t_ref[...] = pltpu.matmul_pop(accs[0]) + pltpu.matmul_pop(accs[1])
        every = jnp.concatenate([hits] * (cells // CELLS), axis=0)
        for n, rhs in enumerate(parts):
            pltpu.matmul_push_rhs(rhs, n // 2, n % 2)
            pltpu.matmul_acc_lhs(accs[n % 2], wt, load_staged_rhs=n // 2)
        v_ref[...] = pltpu.matmul_pop(accs[0]) + pltpu.matmul_pop(accs[1])
        pltpu.matmul_push_rhs(every, 1, 1, transpose=True)
        pltpu.matmul_acc_lhs(accs[1], wt, load_staged_rhs=1)
        g_ref[...] = pltpu.matmul_pop(accs[1])[:, 0:lanes]
    else:
        v_ref[...] = counted(wt, sums)
        every = jnp.concatenate([hits] * nb, axis=0)
        g_ref[...] = lax.dot_general(wt, every, (((1,), (1,)), ((), ())), preferred_element_type=f32)
    power_ref[...] = jnp.sum(sums * sums, axis=0, keepdims=True)
    sub = lax.broadcasted_iota(jnp.int32, (rb, lanes), 0)
    lane = lax.broadcasted_iota(jnp.int32, (rb, lanes), 1)
    mark = (sub == rb - 1) & (lane == (nb - 1) * CELLS)
    for k in range(slots):
        q0 = k * CELLS
        pack = g_ref[q0:q0 + rb, :]
        for i in range(1, nb):
            pack = jnp.where(lane >= i * CELLS, g_ref[q0 + rb * i:q0 + rb * (i + 1), :], pack)
        tile = list_ref[k]
        place = jnp.where(tile >= 0, lax.rem(place_ref[jnp.maximum(tile, 0)], rows_owned), -1)
        pack = jnp.where(mark, place.astype(f32), pack)
        for f in range(feeds):
            pay_ref[f * slots + k, CELLS:CELLS + rb, :] = pack
        for f in range(0, feeds, 2):
            binned = t_ref[q0:q0 + CELLS, f * width:(f + 2) * width]
            crossed = turn(v_ref[q0:q0 + CELLS, f * width:(f + 2) * width], width)
            pay_ref[f * slots + k, 0:CELLS, :] = pair_up(binned, crossed)
            pay_ref[(f + 1) * slots + k, 0:CELLS, :] = pair_up(crossed, binned)
    extra.wait()


def turn(value, shift):
    lanes = value.shape[1]
    shift = shift % lanes
    if shift == 0:
        return value
    if lanes % 128 == 0:
        return pltpu.roll(value, shift, 1)
    return jnp.concatenate([value[:, lanes - shift:], value[:, :lanes - shift]], axis=1)


def gram_blocks(packs):
    rb, lanes = packs[0].shape
    nb = lanes // CELLS
    lane = lax.broadcasted_iota(jnp.int32, (rb, lanes), 1)
    blocks = []
    for first in range(0, len(packs), nb):
        rows = []
        for j in range(nb):
            inside = (lane >= j * CELLS) & (lane < (j + 1) * CELLS)
            for i in range(nb):
                rows.append(jnp.where(inside, turn(packs[first + j], (j - i) * CELLS), 0.0))
        blocks.append(jnp.concatenate(rows, axis=0))
    return blocks


def stacked(block):
    return jnp.concatenate(split3(block), axis=0)


def gram_times(stack, value):
    n = stack.shape[1]
    total = None
    for j, part in enumerate(split3(value)):
        term = jnp.dot(stack[0:(3 - j) * n], part, preferred_element_type=f32)
        for i in range(3 - j):
            piece = term[i * n:(i + 1) * n]
            total = piece if total is None else total + piece
    return total


def gram_times_narrow(stack, value):
    n = stack.shape[1]
    w = value.shape[1]
    wide = jnp.dot(stack, jnp.concatenate(split3(value), axis=1), preferred_element_type=f32)
    wide = wide[2 * n:3 * n] + wide[n:2 * n] + wide[0:n]
    return wide[:, 2 * w:3 * w] + wide[:, w:2 * w] + wide[:, 0:w]


def owner_kernel(
    recv_ref, prior_ref, power_ref,
    pay_ref, map_ref,
    index_ref, even_ref, odd_ref, image_ref,
    *, feeds, rows_owned, samples, rows_out,
):
    sources, rows, lanes = recv_ref.shape
    width = lanes // 2
    nb = lanes // CELLS
    rb = CELLS // nb
    share = rb // feeds
    mark_row = CELLS + rb - 1
    mark_lane = (nb - 1) * CELLS
    feed = lax.axis_index("feed")
    flip = lax.rem(feed, 2) == 1

    def each(body):
        if sources <= 64:
            for d in range(0, sources, 2):
                body(d)
        else:
            lax.fori_loop(0, sources // 2, lambda g, c: (body(2 * g), c)[1], 0)

    def note(d):
        for e in range(2):
            at = recv_ref[d + e, mark_row:mark_row + 1, mark_lane:mark_lane + 1]
            index_ref[d + e] = jnp.max(at.astype(jnp.int32))

    def gather(d):
        for e, ref in enumerate((even_ref, odd_ref)):
            r = jnp.maximum(index_ref[d + e], 0)
            ref[r] += recv_ref[d + e]

    each(note)
    even_ref[...] = jnp.zeros(even_ref.shape, f32)
    odd_ref[...] = jnp.zeros(odd_ref.shape, f32)
    each(gather)
    sub = lax.broadcasted_iota(jnp.int32, (rb, lanes), 0)
    lane = lax.broadcasted_iota(jnp.int32, (rb, lanes), 1)
    mark = (sub == rb - 1) & (lane == mark_lane)
    packs = []
    for r in range(rows_owned):
        pack = even_ref[r, CELLS:CELLS + rb, :] + odd_ref[r, CELLS:CELLS + rb, :]
        packs.append(jnp.where(mark, pack[0:1, CELLS - 1:CELLS], pack))
    prior = prior_ref[...]
    offset = prior - shift_of(prior)
    mine = offset[:, 0:width]
    for f in range(1, feeds):
        mine = jnp.where(feed == f, offset[:, f * width:(f + 1) * width], mine)
    rr = rz = zz = zw = None
    cross = half = last = None
    for g, block in enumerate(gram_blocks(packs)):
        stack = stacked(block)
        hits = jnp.sum(block, axis=1, keepdims=True) / float(samples)
        inverse = 1.0 / jnp.maximum(hits, 1.0)
        members = range(g * nb, (g + 1) * nb)
        both = jnp.concatenate(
            [even_ref[r, 0:CELLS, :] + odd_ref[r, 0:CELLS, :] for r in members], axis=0
        )
        other = turn(both, width)
        v_sum = jnp.where(flip, both, other)[:, 0:width]
        y0 = jnp.where(flip, other, both)[:, 0:width] * inverse
        u0 = v_sum - gram_times_narrow(stack, y0)
        y1 = u0 * inverse
        uz = mine * u0 - gram_times_narrow(stack, y1)
        y2 = uz * inverse
        q0 = g * nb * CELLS
        map_ref[0, q0:q0 + nb * CELLS, :] = y0
        map_ref[1, q0:q0 + nb * CELLS, :] = y1
        map_ref[2, q0:q0 + nb * CELLS, :] = y2
        both = jnp.concatenate([jnp.where(flip, y1, y0), jnp.where(flip, y0, y1)], axis=1)
        for n, r in enumerate(members):
            image_ref[r, 0:CELLS, :] = both[n * CELLS:(n + 1) * CELLS]
        terms = [
            jnp.sum(term, axis=0, keepdims=True)
            for term in (y0 * (v_sum + u0), u0 * y1, y1 * (mine * u0 + uz), uz * y2)
        ]
        if g == 0:
            rr, cross, half, last = terms
        else:
            rr, cross, half, last = rr + terms[0], cross + terms[1], half + terms[2], last + terms[3]
    rr = -rr
    rz = mine * rr - cross
    zz = mine * mine * rr - half
    zw = mine * zz - last
    power = power_ref[...]
    parts = []
    for own in (rr, rz, zz, zw):
        for f in range(feeds):
            own = own + power[:, f * width:(f + 1) * width]
        parts.append(own[:, 0:width // 2] + own[:, width // 2:width])
        power = power * offset
    scal = jnp.concatenate(parts, axis=1)
    fill = jnp.zeros((8 - share - 1, lanes), f32)
    for r in range(rows_owned):
        quarter = packs[r][0:share]
        for f in range(1, feeds):
            quarter = jnp.where(feed == f, packs[r][f * share:(f + 1) * share], quarter)
        image_ref[r, CELLS:CELLS + 8, :] = jnp.concatenate([quarter, scal, fill], axis=0)

    def scatter(d):
        for e in range(2):
            r = jnp.maximum(index_ref[d + e], 0)
            pay_ref[pl.ds((d + e) * rows_out, rows_out), :] = image_ref[r, 0:rows_out, :]

    each(scatter)


def final_kernel(
    recv_ref, prior_ref, sums_ref, w_ref, maps_ref,
    x_out, r_out, sky_out,
    y0_ref, y1_ref, y2_ref, x_ref, r_ref, sky_ref, sems,
    *, slots, feeds, samples, share, rows_in,
):
    lanes = recv_ref.shape[1]
    sources = recv_ref.shape[0] // rows_in
    width = lanes // 2
    nb = lanes // CELLS
    prior = prior_ref[...]
    mean = shift_of(prior)
    offset = prior - mean
    sigma = mean + float(samples)
    scal = None
    for d in range(sources):
        now = recv_ref[d * rows_in + CELLS + share:d * rows_in + CELLS + share + 1, :]
        scal = now if scal is None else scal + now
    quarter = lanes // 4
    rr0, rz, zz, zw = [
        jnp.sum(scal[:, i * quarter:(i + 1) * quarter], axis=1, keepdims=True) for i in range(4)
    ]
    gamma = rz / rr0
    alpha0 = 1.0 / (sigma + gamma)
    ee = zz - gamma * rz
    rr1 = alpha0 * alpha0 * ee
    beta = rr1 / rr0
    e_a_e = sigma * ee + (zw - 2.0 * gamma * zz + gamma * gamma * rz)
    alpha1 = rr1 / (alpha0 * alpha0 * e_a_e - rr1 * beta / alpha0)
    lead = alpha0 * gamma + beta
    slack = 1.0 - alpha1 * sigma
    x_r = alpha0 + alpha1 * lead
    x_z = -alpha0 * alpha1
    r_r = alpha0 * gamma * slack - alpha1 * sigma * beta
    r_z = -alpha0 * slack - alpha1 * lead
    r_w = alpha0 * alpha1
    packs = []
    for k in range(slots):
        base = [(f * slots + k) * rows_in for f in range(feeds)]
        packs.append(
            jnp.concatenate([recv_ref[b + CELLS:b + CELLS + share, :] for b in base], axis=0)
        )
        q0 = k * CELLS
        for f in range(0, feeds, 2):
            low = recv_ref[base[f]:base[f] + CELLS, :]
            high = recv_ref[base[f + 1]:base[f + 1] + CELLS, :]
            y0_ref[q0:q0 + CELLS, f * width:(f + 2) * width] = pair_up(low, high)
            y1_ref[q0:q0 + CELLS, f * width:(f + 2) * width] = turn(pair_up(high, low), width)
    y0 = y0_ref[...]
    y1 = y1_ref[...]
    sums = sums_ref[...]
    w = w_ref[...]
    lead_x = x_r + x_z * offset
    x_ref[...] = lead_x * sums - counted(w, lead_x * y0 + x_z * y1)
    sky_ref[...] = maps_ref[0] - x_r * maps_ref[1] - x_z * maps_ref[2]
    outs = [
        pltpu.make_async_copy(x_ref, x_out, sems.at[0]),
        pltpu.make_async_copy(sky_ref, sky_out, sems.at[1]),
        pltpu.make_async_copy(r_ref, r_out, sems.at[2]),
    ]
    outs[0].start()
    outs[1].start()
    for g, block in enumerate(gram_blocks(packs)):
        stack = stacked(block)
        hits = jnp.sum(block, axis=1, keepdims=True) / float(samples)
        inverse = 1.0 / jnp.maximum(hits, 1.0)
        q0 = g * nb * CELLS
        part = y1_ref[q0:q0 + nb * CELLS, :]
        y2_ref[q0:q0 + nb * CELLS, :] = offset * part - inverse * gram_times(stack, part)
    second = r_z + r_w * offset
    lead_r = r_r + second * offset
    r_ref[...] = lead_r * sums - counted(w, lead_r * y0 + second * y1 + r_w * y2_ref[...])
    outs[2].start()
    for out in outs:
        out.wait()


def local(tod, pixels, block_slots, tile_lists, tile_place, prior):
    axes = ("feed", "tm")
    feeds = lax.axis_size("feed")
    owners = lax.axis_size("tm")
    slots = tile_lists.shape[1] * tile_lists.shape[2]
    assert slots == owners and feeds % 2 == 0
    rows_owned = tile_place.shape[0] // owners
    blocks, samples, channels = tod.shape
    cells = slots * CELLS
    width = channels // feeds
    lanes = 2 * width
    gram_rows = CELLS * CELLS // lanes
    rows = CELLS + gram_rows
    devices = feeds * owners
    chunk = max(n for n in range(1, 11) if samples % n == 0)
    small = devices * rows * lanes <= 1 << 18
    held = pltpu.VMEM if small else jax.ShapeDtypeStruct
    accs = []
    if blocks == cells == channels == 256 and chunk > 1:
        accs = [pltpu.ACC(n)((cells, channels), f32) for n in range(2)]
    smem = pl.BlockSpec(memory_space=pltpu.SMEM)
    vmem = pl.BlockSpec(memory_space=pltpu.VMEM)

    hbm = pl.BlockSpec(memory_space=pl.ANY)
    payload, sums, weights, power, prior_row = pl.pallas_call(
        lambda *refs: pl.run_scoped(
            functools.partial(
                bin_kernel, *refs, slots=slots, feeds=feeds, rows_owned=rows_owned, chunk=chunk
            ),
            *accs,
        ),
        in_specs=[smem, smem, vmem, vmem, hbm, hbm],
        out_specs=[vmem, vmem, vmem, vmem, vmem],
        out_shape=[
            held((devices, rows, lanes), f32),
            held((blocks, channels), f32),
            held((blocks, cells), bf16),
            held((1, channels), f32),
            held((1, channels), f32),
        ],
        scratch_shapes=[
            pltpu.VMEM((samples, blocks, channels), bf16),
            pltpu.VMEM((cells, blocks), bf16),
            pltpu.VMEM((cells, channels), f32),
            pltpu.VMEM((cells, channels), f32),
            pltpu.VMEM((cells, lanes), f32),
            pltpu.SemaphoreType.DMA,
            pltpu.SemaphoreType.DMA((samples // chunk,)),
        ],
        name="bin_samples",
    )(
        tile_lists.reshape(slots),
        tile_place,
        block_slots.reshape(1, blocks),
        pixels.T,
        prior.reshape(1, channels),
        tod.transpose(1, 0, 2),
    )
    received = lax.all_to_all(payload, axes, split_axis=0, concat_axis=0, tiled=True)
    owned_cells = rows_owned * CELLS
    share = gram_rows // feeds
    rows_back = CELLS + share + 1
    if not small:
        rows_back = -(-rows_back // 8) * 8
    answer, maps = pl.pallas_call(
        lambda *refs: owner_kernel(
            *refs, feeds=feeds, rows_owned=rows_owned, samples=samples, rows_out=rows_back
        ),
        in_specs=[vmem, vmem, vmem],
        out_specs=[vmem, vmem],
        out_shape=[
            held((devices * rows_back, lanes), f32),
            held((3, owned_cells, width), f32),
        ],
        scratch_shapes=[
            pltpu.SMEM((devices,), jnp.int32),
            pltpu.VMEM((rows_owned, rows, lanes), f32),
            pltpu.VMEM((rows_owned, rows, lanes), f32),
            pltpu.VMEM((rows_owned, CELLS + 8, lanes), f32),
        ],
        name="solve_tiles",
    )(near(received, small), near(prior_row, small), near(power, small))
    returned = lax.all_to_all(
        answer.reshape(devices, 1, rows_back * lanes), axes, split_axis=0, concat_axis=0, tiled=True
    ).reshape(devices * rows_back, lanes)
    drift, leftover, sky = pl.pallas_call(
        lambda *refs: final_kernel(
            *refs, slots=slots, feeds=feeds, samples=samples, share=share, rows_in=rows_back
        ),
        in_specs=[vmem, vmem, vmem, vmem, vmem],
        out_specs=[hbm, hbm, hbm],
        out_shape=[
            jax.ShapeDtypeStruct((blocks, channels), f32),
            jax.ShapeDtypeStruct((blocks, channels), f32),
            jax.ShapeDtypeStruct((owned_cells, width), f32),
        ],
        scratch_shapes=[
            pltpu.VMEM((cells, channels), f32),
            pltpu.VMEM((cells, channels), f32),
            pltpu.VMEM((cells, channels), f32),
            pltpu.VMEM((blocks, channels), f32),
            pltpu.VMEM((blocks, channels), f32),
            pltpu.VMEM((owned_cells, width), f32),
            pltpu.SemaphoreType.DMA((3,)),
        ],
        name="finish",
    )(near(returned, small), near(prior_row, small), near(sums, small), near(weights, small), near(maps, small))
    return drift, leftover, sky.reshape(rows_owned, CELLS, width)


def solution(mesh):
    return jax.shard_map(
        local,
        mesh=mesh,
        in_specs=(
            P(("feed", "tm"), None, None),
            P(("feed", "tm"), None),
            P(("feed", "tm")),
            P(("feed", "tm"), None, None),
            P(),
            P(),
        ),
        out_specs=(P(("feed", "tm"), None), P(("feed", "tm"), None), P("tm", None, "feed")),
        check_vma=False,
    )
```

```python
import functools

import jax
import jax.numpy as jnp
from jax import lax
from jax.experimental import pallas as pl
from jax.experimental.pallas import tpu as pltpu
from jax.sharding import PartitionSpec as P

CELLS = 32
EXACT = lax.Precision.HIGHEST
f32 = jnp.float32
bf16 = jnp.bfloat16


def split3(value):
    high = value.astype(bf16)
    rest = value - high.astype(f32)
    mid = rest.astype(bf16)
    low = (rest - mid.astype(f32)).astype(bf16)
    return high, mid, low


def counted(counts, value):
    out = None
    for part in split3(value):
        term = jnp.dot(counts, part, preferred_element_type=f32)
        out = term if out is None else out + term
    return out


def near(value, small):
    return pltpu.with_memory_space_constraint(value, pltpu.VMEM) if small else value


def shift_of(prior):
    return jnp.sum(prior, axis=1, keepdims=True) * (1.0 / prior.shape[1])


def pair_up(low, high):
    lane = lax.broadcasted_iota(jnp.int32, low.shape, 1)
    return jnp.where(lane < low.shape[1] // 2, low, high)


def mark_place(compact, rows, lanes):
    if compact:
        return (rows - 1, 4), (rows - 2, 5)
    return (rows - 1, lanes - CELLS), (0, CELLS - 1)


def mark_of(rows, lanes, compact):
    at = mark_place(compact, rows, lanes)[0]
    sub = lax.broadcasted_iota(jnp.int32, (rows, lanes), 0)
    lane = lax.broadcasted_iota(jnp.int32, (rows, lanes), 1)
    return (sub == at[0]) & (lane == at[1])


def bin_kernel(
    list_ref, place_ref, slot_ref, pix_ref, prior_ref, tod_ref,
    pay_ref, sums_ref, w_ref, prior_out,
    tod_buf, t_ref, v_ref, g_ref, prior_sem, sems, *accs,
    slots, feeds, rows_owned, chunk, compact,
):
    samples, blocks, channels = tod_ref.shape
    cells = slots * CELLS
    lanes = pay_ref.shape[1]
    rows = pay_ref.shape[0] // (feeds * slots)
    width = lanes // 2
    nb = lanes // CELLS
    rb = CELLS // nb
    chunks = samples // chunk
    copies = [
        pltpu.make_async_copy(
            tod_ref.at[pl.ds(i * chunk, chunk)], tod_buf.at[pl.ds(i * chunk, chunk)], sems.at[i]
        )
        for i in range(chunks)
    ]
    for copy in copies:
        copy.start()
    extra = pltpu.make_async_copy(prior_ref, prior_out, prior_sem)
    extra.start()
    one = jnp.ones((), bf16)
    nil = jnp.zeros((), bf16)
    owner = jnp.broadcast_to(slot_ref[...], (16, blocks))
    row = lax.broadcasted_iota(jnp.int32, (16, blocks), 0)
    masks = [(owner == k).astype(f32).astype(bf16) for k in range(slots)]
    halves = [(row + q).astype(f32).astype(bf16) for q in range(0, CELLS, 16)]
    counts = [None] * len(halves)

    def hot_of(s):
        spread = jnp.broadcast_to(pix_ref[s:s + 1, :].astype(f32).astype(bf16), (16, blocks))
        hots = [jnp.where(half == spread, one, nil) for half in halves]
        for h, hot in enumerate(hots):
            counts[h] = hot if counts[h] is None else counts[h] + hot
        return jnp.concatenate([hot * masks[k] for k in range(slots) for hot in hots], axis=0)

    strips = range(0, blocks, 16)

    def add_strip(i, at):
        total = sums_ref[at:at + 16, :] if i else None
        for s in range(i * chunk, (i + 1) * chunk):
            part = tod_buf[s, at:at + 16, :].astype(f32)
            total = part if total is None else total + part
        sums_ref[at:at + 16, :] = total

    if accs:
        def push(s):
            pltpu.matmul_push_rhs(tod_buf[s], s // 2 % 2, s % 2)

        for i in range(chunks):
            copies[i].wait()
            first = i * chunk
            push(first)
            push(first + 1)
            done = 0
            for s in range(first, first + chunk):
                hot = hot_of(s)
                if s + 2 < first + chunk:
                    push(s + 2)
                pltpu.matmul_acc_lhs(accs[s % 2], hot, load_staged_rhs=s // 2 % 2)
                upto = len(strips) * (s + 1 - first) // chunk
                for at in strips[done:upto]:
                    add_strip(i, at)
                done = upto
    else:
        for i in range(chunks):
            copies[i].wait()
            first = i * chunk
            hot = jnp.concatenate([hot_of(s) for s in range(first, first + chunk)], axis=1)
            now = tod_buf[first:first + chunk].reshape(chunk * blocks, channels)
            binned = jnp.dot(hot, now, preferred_element_type=f32)
            t_ref[...] = binned if i == 0 else t_ref[...] + binned
            for at in strips:
                add_strip(i, at)

    hits = jnp.concatenate(counts, axis=0)
    wt = jnp.concatenate(
        [count * masks[k] for k in range(slots) for count in counts], axis=0
    )
    w_ref[...] = wt
    sums = sums_ref[...]
    parts = split3(sums)
    if accs:
        t_ref[...] = pltpu.matmul_pop(accs[0]) + pltpu.matmul_pop(accs[1])
        every = jnp.concatenate([hits] * (cells // CELLS), axis=0)
        for n, rhs in enumerate(parts):
            pltpu.matmul_push_rhs(rhs, n // 2, n % 2)
            pltpu.matmul_acc_lhs(accs[n % 2], wt, load_staged_rhs=n // 2)
        v_ref[...] = pltpu.matmul_pop(accs[0]) + pltpu.matmul_pop(accs[1])
        pltpu.matmul_push_rhs(every, 1, 1, transpose=True)
        pltpu.matmul_acc_lhs(accs[1], wt, load_staged_rhs=1)
        g_ref[...] = pltpu.matmul_pop(accs[1])[:, 0:lanes]
    else:
        v_ref[...] = counted(wt, sums)
        every = jnp.concatenate([hits] * nb, axis=0)
        g_ref[...] = lax.dot_general(wt, every, (((1,), (1,)), ((), ())), preferred_element_type=f32)
    lane = lax.broadcasted_iota(jnp.int32, (rb, lanes), 1)
    mark = mark_of(rows - CELLS, lanes, compact)
    for k in range(slots):
        q0 = k * CELLS
        pack = g_ref[q0:q0 + rb, :]
        for i in range(1, nb):
            pack = jnp.where(lane >= i * CELLS, g_ref[q0 + rb * i:q0 + rb * (i + 1), :], pack)
        tile = list_ref[k]
        place = jnp.where(tile >= 0, lax.rem(place_ref[jnp.maximum(tile, 0)], rows_owned), -1)
        if compact:
            pack = squeeze_pack(pack)
        pack = jnp.where(mark, place.astype(f32), pack)
        for f in range(feeds):
            at = (f * slots + k) * rows + CELLS
            pay_ref[at:at + rows - CELLS, :] = pack
        for f in range(0, feeds, 2):
            binned = t_ref[q0:q0 + CELLS, f * width:(f + 2) * width]
            crossed = turn(v_ref[q0:q0 + CELLS, f * width:(f + 2) * width], width)
            for at, value in (
                ((f * slots + k) * rows, pair_up(binned, crossed)),
                (((f + 1) * slots + k) * rows, pair_up(crossed, binned)),
            ):
                pay_ref[at:at + CELLS, :] = value
    extra.wait()


def turn(value, shift):
    lanes = value.shape[1]
    shift = shift % lanes
    if shift == 0:
        return value
    if lanes % 128 == 0:
        return pltpu.roll(value, shift, 1)
    return jnp.concatenate([value[:, lanes - shift:], value[:, :lanes - shift]], axis=1)


def late(shape, axis):
    return lax.rem(lax.broadcasted_iota(jnp.int32, shape, axis), 8) >= 4


def squeeze_pack(pack):
    low = jnp.where(late((2, 128), 1), pack[4:6], turn(pack, -4)[6:8])
    return jnp.concatenate([pack[0:4], low], axis=0)


def expand_pack(six):
    low = six[4:6]
    rest = jnp.concatenate([low, turn(low, 4)], axis=0)
    return jnp.concatenate([six[0:4], jnp.where(late((4, 128), 1), rest, 0.0)], axis=0)


def gram_blocks(packs, compact):
    if compact:
        blocks = gram_blocks([expand_pack(six) for six in packs], False)
        shape = blocks[0].shape
        mirror = late(shape, 1) & jnp.logical_not(late(shape, 0))
        return [block + jnp.where(mirror, block, 0.0).T for block in blocks]
    rb, lanes = packs[0].shape
    nb = lanes // CELLS
    lane = lax.broadcasted_iota(jnp.int32, (rb, lanes), 1)
    blocks = []
    for first in range(0, len(packs), nb):
        rows = []
        for j in range(nb):
            inside = (lane >= j * CELLS) & (lane < (j + 1) * CELLS)
            for i in range(nb):
                rows.append(jnp.where(inside, turn(packs[first + j], (j - i) * CELLS), 0.0))
        blocks.append(jnp.concatenate(rows, axis=0))
    return blocks


def stacked(block):
    return jnp.concatenate(split3(block), axis=0)


def gram_times(stack, value):
    n = stack.shape[1]
    total = None
    for j, part in enumerate(split3(value)):
        term = jnp.dot(stack[0:(3 - j) * n], part, preferred_element_type=f32)
        for i in range(3 - j):
            piece = term[i * n:(i + 1) * n]
            total = piece if total is None else total + piece
    return total


def gram_times_narrow(stack, value):
    n = stack.shape[1]
    w = value.shape[1]
    wide = jnp.dot(stack, jnp.concatenate(split3(value), axis=1), preferred_element_type=f32)
    wide = wide[2 * n:3 * n] + wide[n:2 * n] + wide[0:n]
    return wide[:, 2 * w:3 * w] + wide[:, w:2 * w] + wide[:, 0:w]


def owner_kernel(
    recv_ref, prior_ref, sums_ref, wt_ref,
    pay_ref, map_ref, w_ref,
    index_ref, even_ref, odd_ref, image_ref,
    *, feeds, rows_owned, samples, rows, rows_out, compact,
):
    sources = recv_ref.shape[0] // rows
    lanes = recv_ref.shape[1]
    width = lanes // 2
    nb = lanes // CELLS
    rb = CELLS // nb
    share = rb // feeds
    gram_rows = rows - CELLS
    marked, mirrored = mark_place(compact, gram_rows, lanes)
    feed = lax.axis_index("feed")
    flip = lax.rem(feed, 2) == 1

    def each(body):
        if sources <= 64:
            for d in range(0, sources, 2):
                body(d)
        else:
            lax.fori_loop(0, sources // 2, lambda g, c: (body(2 * g), c)[1], 0)

    def note(d):
        for e in range(2):
            at = recv_ref[
                pl.ds((d + e) * rows + CELLS + marked[0], 1), marked[1]:marked[1] + 1
            ]
            index_ref[d + e] = jnp.max(at.astype(jnp.int32))

    def gather(d):
        for e, ref in enumerate((even_ref, odd_ref)):
            r = jnp.maximum(index_ref[d + e], 0)
            ref[r] += recv_ref[pl.ds((d + e) * rows, rows), :]

    each(note)
    even_ref[...] = jnp.zeros(even_ref.shape, f32)
    odd_ref[...] = jnp.zeros(odd_ref.shape, f32)
    each(gather)
    mark = mark_of(gram_rows, lanes, compact)
    packs = []
    for r in range(rows_owned):
        pack = even_ref[r, CELLS:rows, :] + odd_ref[r, CELLS:rows, :]
        mirror = pack[mirrored[0]:mirrored[0] + 1, mirrored[1]:mirrored[1] + 1]
        packs.append(jnp.where(mark, mirror, pack))
    prior = prior_ref[...]
    offset = prior - shift_of(prior)
    mine = offset[:, 0:width]
    for f in range(1, feeds):
        mine = jnp.where(feed == f, offset[:, f * width:(f + 1) * width], mine)
    rr = rz = zz = zw = None
    cross = half = last = None
    for g, block in enumerate(gram_blocks(packs, compact)):
        stack = stacked(block)
        hits = jnp.sum(block, axis=1, keepdims=True) / float(samples)
        inverse = 1.0 / jnp.maximum(hits, 1.0)
        members = range(g * nb, (g + 1) * nb)
        both = jnp.concatenate(
            [even_ref[r, 0:CELLS, :] + odd_ref[r, 0:CELLS, :] for r in members], axis=0
        )
        other = turn(both, width)
        v_sum = jnp.where(flip, both, other)[:, 0:width]
        y0 = jnp.where(flip, other, both)[:, 0:width] * inverse
        u0 = v_sum - gram_times_narrow(stack, y0)
        y1 = u0 * inverse
        uz = mine * u0 - gram_times_narrow(stack, y1)
        y2 = uz * inverse
        q0 = g * nb * CELLS
        map_ref[0, q0:q0 + nb * CELLS, :] = y0
        map_ref[1, q0:q0 + nb * CELLS, :] = y1
        map_ref[2, q0:q0 + nb * CELLS, :] = y2
        both = jnp.concatenate([jnp.where(flip, y1, y0), jnp.where(flip, y0, y1)], axis=1)
        for n, r in enumerate(members):
            image_ref[r, 0:CELLS, :] = both[n * CELLS:(n + 1) * CELLS]
        terms = [
            jnp.sum(term, axis=0, keepdims=True)
            for term in (y0 * (v_sum + u0), u0 * y1, y1 * (mine * u0 + uz), uz * y2)
        ]
        if g == 0:
            rr, cross, half, last = terms
        else:
            rr, cross, half, last = rr + terms[0], cross + terms[1], half + terms[2], last + terms[3]
    rr = -rr
    rz = mine * rr - cross
    zz = mine * mine * rr - half
    zw = mine * zz - last
    sums = sums_ref[...]
    power = jnp.sum(sums * sums, axis=0, keepdims=True)
    w_ref[...] = wt_ref[...].T
    parts = []
    for own in (rr, rz, zz, zw):
        for f in range(feeds):
            own = own + power[:, f * width:(f + 1) * width]
        own = own[:, 0:width // 2] + own[:, width // 2:width]
        if compact:
            own = own[:, 0:width // 4] + own[:, width // 4:width // 2]
        parts.append(own)
        power = power * offset
    if compact:
        scal = jnp.concatenate(parts + parts, axis=1)
        side = lax.broadcasted_iota(jnp.int32, (1, lanes), 1) >= width
        keep = jnp.where(flip, side.astype(f32), 1.0 - side.astype(f32)) > 0.5
        for r in range(rows_owned):
            six = packs[r]
            row = six[0:1]
            for f in range(1, feeds):
                row = jnp.where(feed == f, six[f:f + 1], row)
            half_row = jnp.where(feed >= 2, six[5:6], six[4:5])
            image_ref[r, CELLS:CELLS + 2, :] = jnp.concatenate(
                [row, jnp.where(keep, half_row, scal)], axis=0
            )
    else:
        scal = jnp.concatenate(parts, axis=1)
        fill = jnp.zeros((8 - share - 1, lanes), f32)
    for r in range(0 if compact else rows_owned):
        quarter = packs[r][0:share]
        for f in range(1, feeds):
            quarter = jnp.where(feed == f, packs[r][f * share:(f + 1) * share], quarter)
        image_ref[r, CELLS:CELLS + 8, :] = jnp.concatenate([quarter, scal, fill], axis=0)

    def scatter(d):
        for e in range(2):
            r = jnp.maximum(index_ref[d + e], 0)
            pay_ref[pl.ds((d + e) * rows_out, rows_out), :] = image_ref[r, 0:rows_out, :]

    each(scatter)


def final_kernel(
    recv_ref, prior_ref, sums_ref, w_ref, maps_ref,
    x_out, r_out, sky_out,
    y0_ref, y1_ref, y2_ref, x_ref, r_ref, sky_ref, sems,
    *, slots, feeds, samples, share, rows_in, compact,
):
    lanes = recv_ref.shape[1]
    sources = recv_ref.shape[0] // rows_in
    width = lanes // 2
    nb = lanes // CELLS
    prior = prior_ref[...]
    mean = shift_of(prior)
    offset = prior - mean
    sigma = mean + float(samples)
    sides = [None, None]
    for d in range(sources):
        at = d * rows_in + CELLS + share
        side = d // slots % 2 if compact else 0
        now = recv_ref[at:at + 1, :]
        sides[side] = now if sides[side] is None else sides[side] + now
    scal = sides[0][:, width:lanes] + sides[1][:, 0:width] if compact else sides[0]
    quarter = scal.shape[1] // 4
    rr0, rz, zz, zw = [
        jnp.sum(scal[:, i * quarter:(i + 1) * quarter], axis=1, keepdims=True) for i in range(4)
    ]
    gamma = rz / rr0
    alpha0 = 1.0 / (sigma + gamma)
    ee = zz - gamma * rz
    rr1 = alpha0 * alpha0 * ee
    beta = rr1 / rr0
    e_a_e = sigma * ee + (zw - 2.0 * gamma * zz + gamma * gamma * rz)
    alpha1 = rr1 / (alpha0 * alpha0 * e_a_e - rr1 * beta / alpha0)
    lead = alpha0 * gamma + beta
    slack = 1.0 - alpha1 * sigma
    x_r = alpha0 + alpha1 * lead
    x_z = -alpha0 * alpha1
    r_r = alpha0 * gamma * slack - alpha1 * sigma * beta
    r_z = -alpha0 * slack - alpha1 * lead
    r_w = alpha0 * alpha1
    packs = []
    for k in range(slots):
        base = [(f * slots + k) * rows_in for f in range(feeds)]
        pieces = [recv_ref[b + CELLS:b + CELLS + share, :] for b in base]
        if compact:
            ends = [recv_ref[b + CELLS + 1:b + CELLS + 2, :] for b in base]
            pieces += [pair_up(ends[0], ends[1]), pair_up(ends[2], ends[3])]
        packs.append(jnp.concatenate(pieces, axis=0))
        q0 = k * CELLS
        for f in range(0, feeds, 2):
            low = recv_ref[base[f]:base[f] + CELLS, :]
            high = recv_ref[base[f + 1]:base[f + 1] + CELLS, :]
            y0_ref[q0:q0 + CELLS, f * width:(f + 2) * width] = pair_up(low, high)
            y1_ref[q0:q0 + CELLS, f * width:(f + 2) * width] = turn(pair_up(high, low), width)
    y0 = y0_ref[...]
    y1 = y1_ref[...]
    sums = sums_ref[...]
    w = w_ref[...]
    lead_x = x_r + x_z * offset
    x_ref[...] = lead_x * sums - counted(w, lead_x * y0 + x_z * y1)
    sky_ref[...] = maps_ref[0] - x_r * maps_ref[1] - x_z * maps_ref[2]
    outs = [
        pltpu.make_async_copy(x_ref, x_out, sems.at[0]),
        pltpu.make_async_copy(sky_ref, sky_out, sems.at[1]),
        pltpu.make_async_copy(r_ref, r_out, sems.at[2]),
    ]
    outs[0].start()
    outs[1].start()
    for g, block in enumerate(gram_blocks(packs, compact)):
        stack = stacked(block)
        hits = jnp.sum(block, axis=1, keepdims=True) / float(samples)
        inverse = 1.0 / jnp.maximum(hits, 1.0)
        q0 = g * nb * CELLS
        part = y1_ref[q0:q0 + nb * CELLS, :]
        y2_ref[q0:q0 + nb * CELLS, :] = offset * part - inverse * gram_times(stack, part)
    second = r_z + r_w * offset
    lead_r = r_r + second * offset
    r_ref[...] = lead_r * sums - counted(w, lead_r * y0 + second * y1 + r_w * y2_ref[...])
    outs[2].start()
    for out in outs:
        out.wait()


def local(tod, pixels, block_slots, tile_lists, tile_place, prior):
    axes = ("feed", "tm")
    feeds = lax.axis_size("feed")
    owners = lax.axis_size("tm")
    slots = tile_lists.shape[1] * tile_lists.shape[2]
    assert slots == owners and feeds % 2 == 0
    rows_owned = tile_place.shape[0] // owners
    blocks, samples, channels = tod.shape
    cells = slots * CELLS
    width = channels // feeds
    lanes = 2 * width
    compact = lanes == 128 and feeds == 4
    gram_rows = 6 if compact else CELLS * CELLS // lanes
    rows = CELLS + gram_rows
    devices = feeds * owners
    chunk = max(n for n in range(1, 11) if samples % n == 0)
    small = devices * rows * lanes <= 1 << 18
    held = pltpu.VMEM if small else jax.ShapeDtypeStruct
    accs = []
    if blocks == cells == channels == 256 and chunk > 1:
        accs = [pltpu.ACC(n)((cells, channels), f32) for n in range(2)]
    smem = pl.BlockSpec(memory_space=pltpu.SMEM)
    vmem = pl.BlockSpec(memory_space=pltpu.VMEM)

    hbm = pl.BlockSpec(memory_space=pl.ANY)
    payload, sums, counts, prior_row = pl.pallas_call(
        lambda *refs: pl.run_scoped(
            functools.partial(
                bin_kernel, *refs, slots=slots, feeds=feeds, rows_owned=rows_owned, chunk=chunk,
                compact=compact,
            ),
            *accs,
        ),
        in_specs=[smem, smem, vmem, vmem, hbm, hbm],
        out_specs=[vmem, vmem, vmem, vmem],
        out_shape=[
            held((devices * rows, lanes), f32),
            held((blocks, channels), f32),
            held((cells, blocks), bf16),
            held((1, channels), f32),
        ],
        scratch_shapes=[
            pltpu.VMEM((samples, blocks, channels), bf16),
            pltpu.VMEM((cells, channels), f32),
            pltpu.VMEM((cells, channels), f32),
            pltpu.VMEM((cells, lanes), f32),
            pltpu.SemaphoreType.DMA,
            pltpu.SemaphoreType.DMA((samples // chunk,)),
        ],
        name="bin_samples",
    )(
        tile_lists.reshape(slots),
        tile_place,
        block_slots.reshape(1, blocks),
        pixels.T,
        prior.reshape(1, channels),
        tod.transpose(1, 0, 2),
    )
    received = lax.all_to_all(
        payload.reshape(devices, 1, rows * lanes), axes, split_axis=0, concat_axis=0, tiled=True
    ).reshape(devices * rows, lanes)
    owned_cells = rows_owned * CELLS
    share = 1 if compact else gram_rows // feeds
    rows_back = CELLS + share + 1
    if not compact:
        rows_back = -(-rows_back // 8) * 8
    answer, maps, weights = pl.pallas_call(
        lambda *refs: owner_kernel(
            *refs, feeds=feeds, rows_owned=rows_owned, samples=samples, rows=rows,
            rows_out=rows_back, compact=compact
        ),
        in_specs=[vmem, vmem, vmem, vmem],
        out_specs=[vmem, vmem, vmem],
        out_shape=[
            held((devices * rows_back, lanes), f32),
            held((3, owned_cells, width), f32),
            held((blocks, cells), bf16),
        ],
        scratch_shapes=[
            pltpu.SMEM((devices,), jnp.int32),
            pltpu.VMEM((rows_owned, rows, lanes), f32),
            pltpu.VMEM((rows_owned, rows, lanes), f32),
            pltpu.VMEM((rows_owned, CELLS + 8, lanes), f32),
        ],
        name="solve_tiles",
    )(near(received, small), near(prior_row, small), near(sums, small), near(counts, small))
    returned = lax.all_to_all(
        answer.reshape(devices, 1, rows_back * lanes), axes, split_axis=0, concat_axis=0, tiled=True
    ).reshape(devices * rows_back, lanes)
    drift, leftover, sky = pl.pallas_call(
        lambda *refs: final_kernel(
            *refs, slots=slots, feeds=feeds, samples=samples, share=share, rows_in=rows_back,
            compact=compact,
        ),
        in_specs=[vmem, vmem, vmem, vmem, vmem],
        out_specs=[hbm, hbm, hbm],
        out_shape=[
            jax.ShapeDtypeStruct((blocks, channels), f32),
            jax.ShapeDtypeStruct((blocks, channels), f32),
            jax.ShapeDtypeStruct((owned_cells, width), f32),
        ],
        scratch_shapes=[
            pltpu.VMEM((cells, channels), f32),
            pltpu.VMEM((cells, channels), f32),
            pltpu.VMEM((cells, channels), f32),
            pltpu.VMEM((blocks, channels), f32),
            pltpu.VMEM((blocks, channels), f32),
            pltpu.VMEM((owned_cells, width), f32),
            pltpu.SemaphoreType.DMA((3,)),
        ],
        name="finish",
    )(near(returned, small), near(prior_row, small), near(sums, small), near(weights, small), near(maps, small))
    return drift, leftover, sky.reshape(rows_owned, CELLS, width)


def solution(mesh):
    return jax.shard_map(
        local,
        mesh=mesh,
        in_specs=(
            P(("feed", "tm"), None, None),
            P(("feed", "tm"), None),
            P(("feed", "tm")),
            P(("feed", "tm"), None, None),
            P(),
            P(),
        ),
        out_specs=(P(("feed", "tm"), None), P(("feed", "tm"), None), P("tm", None, "feed")),
        check_vma=False,
    )
```

```python
import functools

import jax
import jax.numpy as jnp
from jax import lax
from jax.experimental import pallas as pl
from jax.experimental.pallas import tpu as pltpu
from jax.sharding import PartitionSpec as P

CELLS = 32
EXACT = lax.Precision.HIGHEST
f32 = jnp.float32
bf16 = jnp.bfloat16


def split3(value):
    high = value.astype(bf16)
    rest = value - high.astype(f32)
    mid = rest.astype(bf16)
    low = (rest - mid.astype(f32)).astype(bf16)
    return high, mid, low


def counted(counts, value):
    out = None
    for part in split3(value):
        term = jnp.dot(counts, part, preferred_element_type=f32)
        out = term if out is None else out + term
    return out


def near(value, small):
    return pltpu.with_memory_space_constraint(value, pltpu.VMEM) if small else value


def shift_of(prior):
    return jnp.sum(prior, axis=1, keepdims=True) * (1.0 / prior.shape[1])


def pair_up(low, high):
    lane = lax.broadcasted_iota(jnp.int32, low.shape, 1)
    return jnp.where(lane < low.shape[1] // 2, low, high)


def mark_place(compact, rows, lanes):
    if compact:
        return (rows - 1, 4), (rows - 2, 5)
    return (rows - 1, lanes - CELLS), (0, CELLS - 1)


def mark_of(rows, lanes, compact):
    at = mark_place(compact, rows, lanes)[0]
    sub = lax.broadcasted_iota(jnp.int32, (rows, lanes), 0)
    lane = lax.broadcasted_iota(jnp.int32, (rows, lanes), 1)
    return (sub == at[0]) & (lane == at[1])


def bin_kernel(
    list_ref, place_ref, slot_ref, pix_ref, prior_ref, tod_ref,
    pay_ref, sums_ref, w_ref, prior_out,
    tod_buf, t_ref, v_ref, g_ref, prior_sem, sems, *accs,
    slots, feeds, rows_owned, chunk, compact,
):
    samples, blocks, channels = tod_ref.shape
    cells = slots * CELLS
    lanes = pay_ref.shape[1]
    rows = pay_ref.shape[0] // (feeds * slots)
    width = lanes // 2
    nb = lanes // CELLS
    rb = CELLS // nb
    chunks = samples // chunk
    copies = [
        pltpu.make_async_copy(
            tod_ref.at[pl.ds(i * chunk, chunk)], tod_buf.at[pl.ds(i * chunk, chunk)], sems.at[i]
        )
        for i in range(chunks)
    ]
    for copy in copies:
        copy.start()
    extra = pltpu.make_async_copy(prior_ref, prior_out, prior_sem)
    extra.start()
    one = jnp.ones((), bf16)
    nil = jnp.zeros((), bf16)
    owner = jnp.broadcast_to(slot_ref[...], (16, blocks))
    row = lax.broadcasted_iota(jnp.int32, (16, blocks), 0)
    masks = [(owner == k).astype(f32).astype(bf16) for k in range(slots)]
    halves = [(row + q).astype(f32).astype(bf16) for q in range(0, CELLS, 16)]
    counts = [None] * len(halves)

    def hot_of(s):
        spread = jnp.broadcast_to(pix_ref[s:s + 1, :].astype(f32).astype(bf16), (16, blocks))
        hots = [jnp.where(half == spread, one, nil) for half in halves]
        for h, hot in enumerate(hots):
            counts[h] = hot if counts[h] is None else counts[h] + hot
        return jnp.concatenate([hot * masks[k] for k in range(slots) for hot in hots], axis=0)

    strips = range(0, blocks, 16)

    def add_strip(i, at):
        total = sums_ref[at:at + 16, :] if i else None
        for s in range(i * chunk, (i + 1) * chunk):
            part = tod_buf[s, at:at + 16, :].astype(f32)
            total = part if total is None else total + part
        sums_ref[at:at + 16, :] = total

    if accs:
        def push(s):
            pltpu.matmul_push_rhs(tod_buf[s], s // 2 % 2, s % 2)

        for i in range(chunks):
            copies[i].wait()
            first = i * chunk
            push(first)
            push(first + 1)
            done = 0
            for s in range(first, first + chunk):
                hot = hot_of(s)
                if s + 2 < first + chunk:
                    push(s + 2)
                pltpu.matmul_acc_lhs(accs[s % 2], hot, load_staged_rhs=s // 2 % 2)
                upto = len(strips) * (s + 1 - first) // chunk
                for at in strips[done:upto]:
                    add_strip(i, at)
                done = upto
    else:
        for i in range(chunks):
            copies[i].wait()
            first = i * chunk
            hot = jnp.concatenate([hot_of(s) for s in range(first, first + chunk)], axis=1)
            now = tod_buf[first:first + chunk].reshape(chunk * blocks, channels)
            binned = jnp.dot(hot, now, preferred_element_type=f32)
            t_ref[...] = binned if i == 0 else t_ref[...] + binned
            for at in strips:
                add_strip(i, at)

    hits = jnp.concatenate(counts, axis=0)
    wt = jnp.concatenate(
        [count * masks[k] for k in range(slots) for count in counts], axis=0
    )
    w_ref[...] = wt
    sums = sums_ref[...]
    parts = split3(sums)
    if accs:
        every = jnp.concatenate([hits] * (cells // CELLS), axis=0)
        pltpu.matmul_push_rhs(every, 1, 1, transpose=True)
        pltpu.matmul_acc_lhs(accs[4], wt, load_staged_rhs=1)
        for n, rhs in enumerate(parts):
            pltpu.matmul_push_rhs(rhs, n // 2, n % 2)
            pltpu.matmul_acc_lhs(accs[2 + n % 2], wt, load_staged_rhs=n // 2)
        t_ref[...] = pltpu.matmul_pop(accs[0]) + pltpu.matmul_pop(accs[1])
        g_ref[...] = pltpu.matmul_pop(accs[4])[:, 0:lanes]
        v_ref[...] = pltpu.matmul_pop(accs[2]) + pltpu.matmul_pop(accs[3])
    else:
        v_ref[...] = counted(wt, sums)
        every = jnp.concatenate([hits] * nb, axis=0)
        g_ref[...] = lax.dot_general(wt, every, (((1,), (1,)), ((), ())), preferred_element_type=f32)
    lane = lax.broadcasted_iota(jnp.int32, (rb, lanes), 1)
    mark = mark_of(rows - CELLS, lanes, compact)
    for k in range(slots):
        q0 = k * CELLS
        pack = g_ref[q0:q0 + rb, :]
        for i in range(1, nb):
            pack = jnp.where(lane >= i * CELLS, g_ref[q0 + rb * i:q0 + rb * (i + 1), :], pack)
        tile = list_ref[k]
        place = jnp.where(tile >= 0, lax.rem(place_ref[jnp.maximum(tile, 0)], rows_owned), -1)
        if compact:
            pack = squeeze_pack(pack)
        pack = jnp.where(mark, place.astype(f32), pack)
        for f in range(feeds):
            at = (f * slots + k) * rows + CELLS
            pay_ref[at:at + rows - CELLS, :] = pack
        for f in range(0, feeds, 2):
            binned = t_ref[q0:q0 + CELLS, f * width:(f + 2) * width]
            crossed = turn(v_ref[q0:q0 + CELLS, f * width:(f + 2) * width], width)
            for at, value in (
                ((f * slots + k) * rows, pair_up(binned, crossed)),
                (((f + 1) * slots + k) * rows, pair_up(crossed, binned)),
            ):
                pay_ref[at:at + CELLS, :] = value
    extra.wait()


def turn(value, shift):
    lanes = value.shape[1]
    shift = shift % lanes
    if shift == 0:
        return value
    if lanes % 128 == 0:
        return pltpu.roll(value, shift, 1)
    return jnp.concatenate([value[:, lanes - shift:], value[:, :lanes - shift]], axis=1)


def late(shape, axis):
    return lax.rem(lax.broadcasted_iota(jnp.int32, shape, axis), 8) >= 4


def squeeze_pack(pack):
    low = jnp.where(late((2, 128), 1), pack[4:6], turn(pack, -4)[6:8])
    return jnp.concatenate([pack[0:4], low], axis=0)


def expand_pack(six):
    low = six[4:6]
    rest = jnp.concatenate([low, turn(low, 4)], axis=0)
    return jnp.concatenate([six[0:4], jnp.where(late((4, 128), 1), rest, 0.0)], axis=0)


def gram_blocks(packs, compact):
    if compact:
        blocks = gram_blocks([expand_pack(six) for six in packs], False)
        shape = blocks[0].shape
        mirror = late(shape, 1) & jnp.logical_not(late(shape, 0))
        return [block + jnp.where(mirror, block, 0.0).T for block in blocks]
    rb, lanes = packs[0].shape
    nb = lanes // CELLS
    lane = lax.broadcasted_iota(jnp.int32, (rb, lanes), 1)
    blocks = []
    for first in range(0, len(packs), nb):
        rows = []
        for j in range(nb):
            inside = (lane >= j * CELLS) & (lane < (j + 1) * CELLS)
            for i in range(nb):
                rows.append(jnp.where(inside, turn(packs[first + j], (j - i) * CELLS), 0.0))
        blocks.append(jnp.concatenate(rows, axis=0))
    return blocks


def stacked(block):
    return jnp.concatenate(split3(block), axis=0)


def gram_times(stack, value):
    n = stack.shape[1]
    total = None
    for j, part in enumerate(split3(value)):
        term = jnp.dot(stack[0:(3 - j) * n], part, preferred_element_type=f32)
        for i in range(3 - j):
            piece = term[i * n:(i + 1) * n]
            total = piece if total is None else total + piece
    return total


def gram_times_narrow(stack, value):
    n = stack.shape[1]
    w = value.shape[1]
    wide = jnp.dot(stack, jnp.concatenate(split3(value), axis=1), preferred_element_type=f32)
    wide = wide[2 * n:3 * n] + wide[n:2 * n] + wide[0:n]
    return wide[:, 2 * w:3 * w] + wide[:, w:2 * w] + wide[:, 0:w]


def owner_kernel(
    recv_ref, prior_ref, sums_ref, wt_ref,
    pay_ref, map_ref, w_ref,
    index_ref, even_ref, odd_ref, image_ref,
    *, feeds, rows_owned, samples, rows, rows_out, compact,
):
    sources = recv_ref.shape[0] // rows
    lanes = recv_ref.shape[1]
    width = lanes // 2
    nb = lanes // CELLS
    rb = CELLS // nb
    share = rb // feeds
    gram_rows = rows - CELLS
    marked, mirrored = mark_place(compact, gram_rows, lanes)
    feed = lax.axis_index("feed")
    flip = lax.rem(feed, 2) == 1

    def each(body):
        if sources <= 64:
            for d in range(0, sources, 2):
                body(d)
        else:
            lax.fori_loop(0, sources // 2, lambda g, c: (body(2 * g), c)[1], 0)

    def note(d):
        for e in range(2):
            at = recv_ref[
                pl.ds((d + e) * rows + CELLS + marked[0], 1), marked[1]:marked[1] + 1
            ]
            index_ref[d + e] = jnp.max(at.astype(jnp.int32))

    def gather(d):
        for e, ref in enumerate((even_ref, odd_ref)):
            r = jnp.maximum(index_ref[d + e], 0)
            ref[r] += recv_ref[pl.ds((d + e) * rows, rows), :]

    each(note)
    even_ref[...] = jnp.zeros(even_ref.shape, f32)
    odd_ref[...] = jnp.zeros(odd_ref.shape, f32)
    each(gather)
    mark = mark_of(gram_rows, lanes, compact)
    packs = []
    for r in range(rows_owned):
        pack = even_ref[r, CELLS:rows, :] + odd_ref[r, CELLS:rows, :]
        mirror = pack[mirrored[0]:mirrored[0] + 1, mirrored[1]:mirrored[1] + 1]
        packs.append(jnp.where(mark, mirror, pack))
    prior = prior_ref[...]
    offset = prior - shift_of(prior)
    mine = offset[:, 0:width]
    for f in range(1, feeds):
        mine = jnp.where(feed == f, offset[:, f * width:(f + 1) * width], mine)
    rr = rz = zz = zw = None
    cross = half = last = None
    for g, block in enumerate(gram_blocks(packs, compact)):
        stack = stacked(block)
        hits = jnp.sum(block, axis=1, keepdims=True) / float(samples)
        inverse = 1.0 / jnp.maximum(hits, 1.0)
        members = range(g * nb, (g + 1) * nb)
        both = jnp.concatenate(
            [even_ref[r, 0:CELLS, :] + odd_ref[r, 0:CELLS, :] for r in members], axis=0
        )
        other = turn(both, width)
        v_sum = jnp.where(flip, both, other)[:, 0:width]
        y0 = jnp.where(flip, other, both)[:, 0:width] * inverse
        u0 = v_sum - gram_times_narrow(stack, y0)
        y1 = u0 * inverse
        uz = mine * u0 - gram_times_narrow(stack, y1)
        y2 = uz * inverse
        q0 = g * nb * CELLS
        map_ref[0, q0:q0 + nb * CELLS, :] = y0
        map_ref[1, q0:q0 + nb * CELLS, :] = y1
        map_ref[2, q0:q0 + nb * CELLS, :] = y2
        both = jnp.concatenate([jnp.where(flip, y1, y0), jnp.where(flip, y0, y1)], axis=1)
        for n, r in enumerate(members):
            image_ref[r, 0:CELLS, :] = both[n * CELLS:(n + 1) * CELLS]
        terms = [
            jnp.sum(term, axis=0, keepdims=True)
            for term in (y0 * (v_sum + u0), u0 * y1, y1 * (mine * u0 + uz), uz * y2)
        ]
        if g == 0:
            rr, cross, half, last = terms
        else:
            rr, cross, half, last = rr + terms[0], cross + terms[1], half + terms[2], last + terms[3]
    rr = -rr
    rz = mine * rr - cross
    zz = mine * mine * rr - half
    zw = mine * zz - last
    sums = sums_ref[...]
    power = jnp.sum(sums * sums, axis=0, keepdims=True)
    w_ref[...] = wt_ref[...].T
    parts = []
    for own in (rr, rz, zz, zw):
        for f in range(feeds):
            own = own + power[:, f * width:(f + 1) * width]
        own = own[:, 0:width // 2] + own[:, width // 2:width]
        if compact:
            own = own[:, 0:width // 4] + own[:, width // 4:width // 2]
        parts.append(own)
        power = power * offset
    if compact:
        scal = jnp.concatenate(parts + parts, axis=1)
        side = lax.broadcasted_iota(jnp.int32, (1, lanes), 1) >= width
        keep = jnp.where(flip, side.astype(f32), 1.0 - side.astype(f32)) > 0.5
        for r in range(rows_owned):
            six = packs[r]
            row = six[0:1]
            for f in range(1, feeds):
                row = jnp.where(feed == f, six[f:f + 1], row)
            half_row = jnp.where(feed >= 2, six[5:6], six[4:5])
            image_ref[r, CELLS:CELLS + 2, :] = jnp.concatenate(
                [row, jnp.where(keep, half_row, scal)], axis=0
            )
    else:
        scal = jnp.concatenate(parts, axis=1)
        fill = jnp.zeros((8 - share - 1, lanes), f32)
    for r in range(0 if compact else rows_owned):
        quarter = packs[r][0:share]
        for f in range(1, feeds):
            quarter = jnp.where(feed == f, packs[r][f * share:(f + 1) * share], quarter)
        image_ref[r, CELLS:CELLS + 8, :] = jnp.concatenate([quarter, scal, fill], axis=0)

    def scatter(d):
        for e in range(2):
            r = jnp.maximum(index_ref[d + e], 0)
            pay_ref[pl.ds((d + e) * rows_out, rows_out), :] = image_ref[r, 0:rows_out, :]

    each(scatter)


def final_kernel(
    recv_ref, prior_ref, sums_ref, w_ref, maps_ref,
    x_out, r_out, sky_out,
    y0_ref, y1_ref, y2_ref, x_ref, r_ref, sky_ref, sems,
    *, slots, feeds, samples, share, rows_in, compact,
):
    lanes = recv_ref.shape[1]
    sources = recv_ref.shape[0] // rows_in
    width = lanes // 2
    nb = lanes // CELLS
    prior = prior_ref[...]
    mean = shift_of(prior)
    offset = prior - mean
    sigma = mean + float(samples)
    sides = [None, None]
    for d in range(sources):
        at = d * rows_in + CELLS + share
        side = d // slots % 2 if compact else 0
        now = recv_ref[at:at + 1, :]
        sides[side] = now if sides[side] is None else sides[side] + now
    scal = sides[0][:, width:lanes] + sides[1][:, 0:width] if compact else sides[0]
    quarter = scal.shape[1] // 4
    rr0, rz, zz, zw = [
        jnp.sum(scal[:, i * quarter:(i + 1) * quarter], axis=1, keepdims=True) for i in range(4)
    ]
    gamma = rz / rr0
    alpha0 = 1.0 / (sigma + gamma)
    ee = zz - gamma * rz
    rr1 = alpha0 * alpha0 * ee
    beta = rr1 / rr0
    e_a_e = sigma * ee + (zw - 2.0 * gamma * zz + gamma * gamma * rz)
    alpha1 = rr1 / (alpha0 * alpha0 * e_a_e - rr1 * beta / alpha0)
    lead = alpha0 * gamma + beta
    slack = 1.0 - alpha1 * sigma
    x_r = alpha0 + alpha1 * lead
    x_z = -alpha0 * alpha1
    r_r = alpha0 * gamma * slack - alpha1 * sigma * beta
    r_z = -alpha0 * slack - alpha1 * lead
    r_w = alpha0 * alpha1
    packs = []
    for k in range(slots):
        base = [(f * slots + k) * rows_in for f in range(feeds)]
        pieces = [recv_ref[b + CELLS:b + CELLS + share, :] for b in base]
        if compact:
            ends = [recv_ref[b + CELLS + 1:b + CELLS + 2, :] for b in base]
            pieces += [pair_up(ends[0], ends[1]), pair_up(ends[2], ends[3])]
        packs.append(jnp.concatenate(pieces, axis=0))
        q0 = k * CELLS
        for f in range(0, feeds, 2):
            low = recv_ref[base[f]:base[f] + CELLS, :]
            high = recv_ref[base[f + 1]:base[f + 1] + CELLS, :]
            y0_ref[q0:q0 + CELLS, f * width:(f + 2) * width] = pair_up(low, high)
            y1_ref[q0:q0 + CELLS, f * width:(f + 2) * width] = turn(pair_up(high, low), width)
    y0 = y0_ref[...]
    y1 = y1_ref[...]
    sums = sums_ref[...]
    w = w_ref[...]
    lead_x = x_r + x_z * offset
    x_ref[...] = lead_x * sums - counted(w, lead_x * y0 + x_z * y1)
    sky_ref[...] = maps_ref[0] - x_r * maps_ref[1] - x_z * maps_ref[2]
    outs = [
        pltpu.make_async_copy(x_ref, x_out, sems.at[0]),
        pltpu.make_async_copy(sky_ref, sky_out, sems.at[1]),
        pltpu.make_async_copy(r_ref, r_out, sems.at[2]),
    ]
    outs[0].start()
    outs[1].start()
    for g, block in enumerate(gram_blocks(packs, compact)):
        stack = stacked(block)
        hits = jnp.sum(block, axis=1, keepdims=True) / float(samples)
        inverse = 1.0 / jnp.maximum(hits, 1.0)
        q0 = g * nb * CELLS
        part = y1_ref[q0:q0 + nb * CELLS, :]
        y2_ref[q0:q0 + nb * CELLS, :] = offset * part - inverse * gram_times(stack, part)
    second = r_z + r_w * offset
    lead_r = r_r + second * offset
    r_ref[...] = lead_r * sums - counted(w, lead_r * y0 + second * y1 + r_w * y2_ref[...])
    outs[2].start()
    for out in outs:
        out.wait()


def local(tod, pixels, block_slots, tile_lists, tile_place, prior):
    axes = ("feed", "tm")
    feeds = lax.axis_size("feed")
    owners = lax.axis_size("tm")
    slots = tile_lists.shape[1] * tile_lists.shape[2]
    assert slots == owners and feeds % 2 == 0
    rows_owned = tile_place.shape[0] // owners
    blocks, samples, channels = tod.shape
    cells = slots * CELLS
    width = channels // feeds
    lanes = 2 * width
    compact = lanes == 128 and feeds == 4
    gram_rows = 6 if compact else CELLS * CELLS // lanes
    rows = CELLS + gram_rows
    devices = feeds * owners
    chunk = max(n for n in range(1, 11) if samples % n == 0)
    small = devices * rows * lanes <= 1 << 18
    held = pltpu.VMEM if small else jax.ShapeDtypeStruct
    accs = []
    if blocks == cells == channels == 256 and chunk > 1:
        accs = [pltpu.ACC(n)((cells, channels), f32) for n in (0, 1, 0, 1, 1)]
    smem = pl.BlockSpec(memory_space=pltpu.SMEM)
    vmem = pl.BlockSpec(memory_space=pltpu.VMEM)

    hbm = pl.BlockSpec(memory_space=pl.ANY)
    payload, sums, counts, prior_row = pl.pallas_call(
        lambda *refs: pl.run_scoped(
            functools.partial(
                bin_kernel, *refs, slots=slots, feeds=feeds, rows_owned=rows_owned, chunk=chunk,
                compact=compact,
            ),
            *accs,
        ),
        in_specs=[smem, smem, vmem, vmem, hbm, hbm],
        out_specs=[vmem, vmem, vmem, vmem],
        out_shape=[
            held((devices * rows, lanes), f32),
            held((blocks, channels), f32),
            held((cells, blocks), bf16),
            held((1, channels), f32),
        ],
        scratch_shapes=[
            pltpu.VMEM((samples, blocks, channels), bf16),
            pltpu.VMEM((cells, channels), f32),
            pltpu.VMEM((cells, channels), f32),
            pltpu.VMEM((cells, lanes), f32),
            pltpu.SemaphoreType.DMA,
            pltpu.SemaphoreType.DMA((samples // chunk,)),
        ],
        name="bin_samples",
    )(
        tile_lists.reshape(slots),
        tile_place,
        block_slots.reshape(1, blocks),
        pixels.T,
        prior.reshape(1, channels),
        tod.transpose(1, 0, 2),
    )
    received = lax.all_to_all(
        payload.reshape(devices, 1, rows * lanes), axes, split_axis=0, concat_axis=0, tiled=True
    ).reshape(devices * rows, lanes)
    owned_cells = rows_owned * CELLS
    share = 1 if compact else gram_rows // feeds
    rows_back = CELLS + share + 1
    if not compact:
        rows_back = -(-rows_back // 8) * 8
    answer, maps, weights = pl.pallas_call(
        lambda *refs: owner_kernel(
            *refs, feeds=feeds, rows_owned=rows_owned, samples=samples, rows=rows,
            rows_out=rows_back, compact=compact
        ),
        in_specs=[vmem, vmem, vmem, vmem],
        out_specs=[vmem, vmem, vmem],
        out_shape=[
            held((devices * rows_back, lanes), f32),
            held((3, owned_cells, width), f32),
            held((blocks, cells), bf16),
        ],
        scratch_shapes=[
            pltpu.SMEM((devices,), jnp.int32),
            pltpu.VMEM((rows_owned, rows, lanes), f32),
            pltpu.VMEM((rows_owned, rows, lanes), f32),
            pltpu.VMEM((rows_owned, CELLS + 8, lanes), f32),
        ],
        name="solve_tiles",
    )(near(received, small), near(prior_row, small), near(sums, small), near(counts, small))
    returned = lax.all_to_all(
        answer.reshape(devices, 1, rows_back * lanes), axes, split_axis=0, concat_axis=0, tiled=True
    ).reshape(devices * rows_back, lanes)
    drift, leftover, sky = pl.pallas_call(
        lambda *refs: final_kernel(
            *refs, slots=slots, feeds=feeds, samples=samples, share=share, rows_in=rows_back,
            compact=compact,
        ),
        in_specs=[vmem, vmem, vmem, vmem, vmem],
        out_specs=[hbm, hbm, hbm],
        out_shape=[
            jax.ShapeDtypeStruct((blocks, channels), f32),
            jax.ShapeDtypeStruct((blocks, channels), f32),
            jax.ShapeDtypeStruct((owned_cells, width), f32),
        ],
        scratch_shapes=[
            pltpu.VMEM((cells, channels), f32),
            pltpu.VMEM((cells, channels), f32),
            pltpu.VMEM((cells, channels), f32),
            pltpu.VMEM((blocks, channels), f32),
            pltpu.VMEM((blocks, channels), f32),
            pltpu.VMEM((owned_cells, width), f32),
            pltpu.SemaphoreType.DMA((3,)),
        ],
        name="finish",
    )(near(returned, small), near(prior_row, small), near(sums, small), near(weights, small), near(maps, small))
    return drift, leftover, sky.reshape(rows_owned, CELLS, width)


def solution(mesh):
    return jax.shard_map(
        local,
        mesh=mesh,
        in_specs=(
            P(("feed", "tm"), None, None),
            P(("feed", "tm"), None),
            P(("feed", "tm")),
            P(("feed", "tm"), None, None),
            P(),
            P(),
        ),
        out_specs=(P(("feed", "tm"), None), P(("feed", "tm"), None), P("tm", None, "feed")),
        check_vma=False,
    )
```

```python
import functools

import jax
import jax.numpy as jnp
from jax import lax
from jax.experimental import pallas as pl
from jax.experimental.pallas import tpu as pltpu
from jax.sharding import PartitionSpec as P

CELLS = 32
EXACT = lax.Precision.HIGHEST
f32 = jnp.float32
bf16 = jnp.bfloat16


def split3(value):
    high = value.astype(bf16)
    rest = value - high.astype(f32)
    mid = rest.astype(bf16)
    low = (rest - mid.astype(f32)).astype(bf16)
    return high, mid, low


def counted(counts, value):
    out = None
    for part in split3(value):
        term = jnp.dot(counts, part, preferred_element_type=f32)
        out = term if out is None else out + term
    return out


def near(value, small):
    return pltpu.with_memory_space_constraint(value, pltpu.VMEM) if small else value


def shift_of(prior):
    return jnp.sum(prior, axis=1, keepdims=True) * (1.0 / prior.shape[1])


def pair_up(low, high):
    lane = lax.broadcasted_iota(jnp.int32, low.shape, 1)
    return jnp.where(lane < low.shape[1] // 2, low, high)


def mark_place(compact, rows, lanes):
    if compact:
        return (rows - 1, 4), (rows - 2, 5)
    return (rows - 1, lanes - CELLS), (0, CELLS - 1)


def mark_of(rows, lanes, compact):
    at = mark_place(compact, rows, lanes)[0]
    sub = lax.broadcasted_iota(jnp.int32, (rows, lanes), 0)
    lane = lax.broadcasted_iota(jnp.int32, (rows, lanes), 1)
    return (sub == at[0]) & (lane == at[1])


def bin_kernel(
    list_ref, place_ref, slot_ref, pix_ref, prior_ref, tod_ref,
    pay_ref, sums_ref, w_ref, prior_out,
    tod_buf, t_ref, v_ref, g_ref, prior_sem, sems, *accs,
    slots, feeds, rows_owned, chunk, compact,
):
    samples, blocks, channels = tod_ref.shape
    cells = slots * CELLS
    lanes = pay_ref.shape[1]
    rows = pay_ref.shape[0] // (feeds * slots)
    width = lanes // 2
    nb = lanes // CELLS
    rb = CELLS // nb
    chunks = samples // chunk
    copies = [
        pltpu.make_async_copy(
            tod_ref.at[pl.ds(i * chunk, chunk)], tod_buf.at[pl.ds(i * chunk, chunk)], sems.at[i]
        )
        for i in range(chunks)
    ]
    for copy in copies:
        copy.start()
    extra = pltpu.make_async_copy(prior_ref, prior_out, prior_sem)
    extra.start()
    one = jnp.ones((), bf16)
    nil = jnp.zeros((), bf16)
    owner = jnp.broadcast_to(slot_ref[...], (16, blocks))
    row = lax.broadcasted_iota(jnp.int32, (16, blocks), 0)
    masks = [(owner == k).astype(f32).astype(bf16) for k in range(slots)]
    halves = [(row + q).astype(f32).astype(bf16) for q in range(0, CELLS, 16)]
    counts = [None] * len(halves)

    def hot_of(s):
        spread = jnp.broadcast_to(pix_ref[s:s + 1, :].astype(f32).astype(bf16), (16, blocks))
        hots = [jnp.where(half == spread, one, nil) for half in halves]
        for h, hot in enumerate(hots):
            counts[h] = hot if counts[h] is None else counts[h] + hot
        return jnp.concatenate([hot * masks[k] for k in range(slots) for hot in hots], axis=0)

    strips = range(0, blocks, 16)

    def add_strip(i, at):
        total = sums_ref[at:at + 16, :] if i else None
        for s in range(i * chunk, (i + 1) * chunk):
            part = tod_buf[s, at:at + 16, :].astype(f32)
            total = part if total is None else total + part
        sums_ref[at:at + 16, :] = total

    if accs:
        def push(s):
            pltpu.matmul_push_rhs(tod_buf[s], s // 2 % 2, s % 2)

        for i in range(chunks):
            copies[i].wait()
            first = i * chunk
            push(first)
            push(first + 1)
            done = 0
            for s in range(first, first + chunk):
                hot = hot_of(s)
                if s + 2 < first + chunk:
                    push(s + 2)
                pltpu.matmul_acc_lhs(accs[s % 2], hot, load_staged_rhs=s // 2 % 2)
                upto = len(strips) * (s + 1 - first) // chunk
                for at in strips[done:upto]:
                    add_strip(i, at)
                done = upto
    else:
        for i in range(chunks):
            copies[i].wait()
            first = i * chunk
            hot = jnp.concatenate([hot_of(s) for s in range(first, first + chunk)], axis=1)
            now = tod_buf[first:first + chunk].reshape(chunk * blocks, channels)
            binned = jnp.dot(hot, now, preferred_element_type=f32)
            t_ref[...] = binned if i == 0 else t_ref[...] + binned
            for at in strips:
                add_strip(i, at)

    hits = jnp.concatenate(counts, axis=0)
    wt = jnp.concatenate(
        [count * masks[k] for k in range(slots) for count in counts], axis=0
    )
    w_ref[...] = wt
    sums = sums_ref[...]
    parts = split3(sums)
    if accs:
        every = jnp.concatenate([hits] * (cells // CELLS), axis=0)
        pltpu.matmul_push_rhs(every, 1, 1, transpose=True)
        pltpu.matmul_acc_lhs(accs[4], wt, load_staged_rhs=1)
        for n, rhs in enumerate(parts):
            pltpu.matmul_push_rhs(rhs, n // 2, n % 2)
            pltpu.matmul_acc_lhs(accs[2 + n % 2], wt, load_staged_rhs=n // 2)
        t_ref[...] = pltpu.matmul_pop(accs[0]) + pltpu.matmul_pop(accs[1])
        g_ref[...] = pltpu.matmul_pop(accs[4])[:, 0:lanes]
        v_ref[...] = pltpu.matmul_pop(accs[2]) + pltpu.matmul_pop(accs[3])
    else:
        v_ref[...] = counted(wt, sums)
        every = jnp.concatenate([hits] * nb, axis=0)
        g_ref[...] = lax.dot_general(wt, every, (((1,), (1,)), ((), ())), preferred_element_type=f32)
    lane = lax.broadcasted_iota(jnp.int32, (rb, lanes), 1)
    mark = mark_of(rows - CELLS, lanes, compact)
    for k in range(slots):
        q0 = k * CELLS
        pack = g_ref[q0:q0 + rb, :]
        for i in range(1, nb):
            pack = jnp.where(lane >= i * CELLS, g_ref[q0 + rb * i:q0 + rb * (i + 1), :], pack)
        tile = list_ref[k]
        place = jnp.where(tile >= 0, lax.rem(place_ref[jnp.maximum(tile, 0)], rows_owned), -1)
        if compact:
            pack = squeeze_pack(pack)
        pack = jnp.where(mark, place.astype(f32), pack)
        for f in range(feeds):
            at = (f * slots + k) * rows + CELLS
            pay_ref[at:at + rows - CELLS, :] = pack
        for f in range(0, feeds, 2):
            binned = t_ref[q0:q0 + CELLS, f * width:(f + 2) * width]
            crossed = turn(v_ref[q0:q0 + CELLS, f * width:(f + 2) * width], width)
            for at, value in (
                ((f * slots + k) * rows, pair_up(binned, crossed)),
                (((f + 1) * slots + k) * rows, pair_up(crossed, binned)),
            ):
                pay_ref[at:at + CELLS, :] = value
    extra.wait()


def turn(value, shift):
    lanes = value.shape[1]
    shift = shift % lanes
    if shift == 0:
        return value
    if lanes % 128 == 0:
        return pltpu.roll(value, shift, 1)
    return jnp.concatenate([value[:, lanes - shift:], value[:, :lanes - shift]], axis=1)


def late(shape, axis):
    return lax.rem(lax.broadcasted_iota(jnp.int32, shape, axis), 8) >= 4


def squeeze_pack(pack):
    low = jnp.where(late((2, 128), 1), pack[4:6], turn(pack, -4)[6:8])
    return jnp.concatenate([pack[0:4], low], axis=0)


def expand_pack(six):
    low = six[4:6]
    rest = jnp.concatenate([low, turn(low, 4)], axis=0)
    return jnp.concatenate([six[0:4], jnp.where(late((4, 128), 1), rest, 0.0)], axis=0)


def gram_blocks(packs, compact):
    if compact:
        blocks = gram_blocks([expand_pack(six) for six in packs], False)
        shape = blocks[0].shape
        mirror = late(shape, 1) & jnp.logical_not(late(shape, 0))
        return [block + jnp.where(mirror, block, 0.0).T for block in blocks]
    rb, lanes = packs[0].shape
    nb = lanes // CELLS
    lane = lax.broadcasted_iota(jnp.int32, (rb, lanes), 1)
    blocks = []
    for first in range(0, len(packs), nb):
        rows = []
        for j in range(nb):
            inside = (lane >= j * CELLS) & (lane < (j + 1) * CELLS)
            for i in range(nb):
                rows.append(jnp.where(inside, turn(packs[first + j], (j - i) * CELLS), 0.0))
        blocks.append(jnp.concatenate(rows, axis=0))
    return blocks


def stacked(block):
    return jnp.concatenate(split3(block), axis=0)


def gram_times(stack, value):
    n = stack.shape[1]
    total = None
    for j, part in enumerate(split3(value)):
        term = jnp.dot(stack[0:(3 - j) * n], part, preferred_element_type=f32)
        for i in range(3 - j):
            piece = term[i * n:(i + 1) * n]
            total = piece if total is None else total + piece
    return total


def gram_times_narrow(stack, value):
    n = stack.shape[1]
    w = value.shape[1]
    wide = jnp.dot(stack, jnp.concatenate(split3(value), axis=1), preferred_element_type=f32)
    wide = wide[2 * n:3 * n] + wide[n:2 * n] + wide[0:n]
    return wide[:, 2 * w:3 * w] + wide[:, w:2 * w] + wide[:, 0:w]


def owner_kernel(
    recv_ref, prior_ref, sums_ref, wt_ref,
    pay_ref, map_ref, w_ref,
    index_ref, *banks,
    feeds, rows_owned, samples, rows, rows_out, compact,
):
    *banks, image_ref = banks
    sources = recv_ref.shape[0] // rows
    lanes = recv_ref.shape[1]
    width = lanes // 2
    nb = lanes // CELLS
    rb = CELLS // nb
    share = rb // feeds
    gram_rows = rows - CELLS
    marked, mirrored = mark_place(compact, gram_rows, lanes)
    feed = lax.axis_index("feed")
    flip = lax.rem(feed, 2) == 1

    def each(body):
        if sources <= 64:
            for d in range(0, sources, 4):
                body(d)
        else:
            lax.fori_loop(0, sources // 4, lambda g, c: (body(4 * g), c)[1], 0)

    def note(d):
        for e in range(4):
            at = recv_ref[
                pl.ds((d + e) * rows + CELLS + marked[0], 1), marked[1]:marked[1] + 1
            ]
            index_ref[d + e] = jnp.max(at.astype(jnp.int32))

    def gather(d):
        for e, ref in enumerate(banks):
            r = jnp.maximum(index_ref[d + e], 0)
            ref[r] += recv_ref[pl.ds((d + e) * rows, rows), :]

    def gathered(r, first, last):
        a, b, c, e = [ref[r, first:last, :] for ref in banks]
        return (a + b) + (c + e)

    each(note)
    for ref in banks:
        ref[...] = jnp.zeros(ref.shape, f32)
    each(gather)
    mark = mark_of(gram_rows, lanes, compact)
    packs = []
    for r in range(rows_owned):
        pack = gathered(r, CELLS, rows)
        mirror = pack[mirrored[0]:mirrored[0] + 1, mirrored[1]:mirrored[1] + 1]
        packs.append(jnp.where(mark, mirror, pack))
    prior = prior_ref[...]
    offset = prior - shift_of(prior)
    mine = offset[:, 0:width]
    for f in range(1, feeds):
        mine = jnp.where(feed == f, offset[:, f * width:(f + 1) * width], mine)
    rr = rz = zz = zw = None
    cross = half = last = None
    for g, block in enumerate(gram_blocks(packs, compact)):
        stack = stacked(block)
        hits = jnp.sum(block, axis=1, keepdims=True) / float(samples)
        inverse = 1.0 / jnp.maximum(hits, 1.0)
        members = range(g * nb, (g + 1) * nb)
        both = jnp.concatenate(
            [gathered(r, 0, CELLS) for r in members], axis=0
        )
        other = turn(both, width)
        v_sum = jnp.where(flip, both, other)[:, 0:width]
        y0 = jnp.where(flip, other, both)[:, 0:width] * inverse
        u0 = v_sum - gram_times_narrow(stack, y0)
        y1 = u0 * inverse
        uz = mine * u0 - gram_times_narrow(stack, y1)
        y2 = uz * inverse
        q0 = g * nb * CELLS
        map_ref[0, q0:q0 + nb * CELLS, :] = y0
        map_ref[1, q0:q0 + nb * CELLS, :] = y1
        map_ref[2, q0:q0 + nb * CELLS, :] = y2
        both = jnp.concatenate([jnp.where(flip, y1, y0), jnp.where(flip, y0, y1)], axis=1)
        for n, r in enumerate(members):
            image_ref[r, 0:CELLS, :] = both[n * CELLS:(n + 1) * CELLS]
        terms = [
            jnp.sum(term, axis=0, keepdims=True)
            for term in (y0 * (v_sum + u0), u0 * y1, y1 * (mine * u0 + uz), uz * y2)
        ]
        if g == 0:
            rr, cross, half, last = terms
        else:
            rr, cross, half, last = rr + terms[0], cross + terms[1], half + terms[2], last + terms[3]
    rr = -rr
    rz = mine * rr - cross
    zz = mine * mine * rr - half
    zw = mine * zz - last
    sums = sums_ref[...]
    power = jnp.sum(sums * sums, axis=0, keepdims=True)
    w_ref[...] = wt_ref[...].T
    parts = []
    for own in (rr, rz, zz, zw):
        for f in range(feeds):
            own = own + power[:, f * width:(f + 1) * width]
        own = own[:, 0:width // 2] + own[:, width // 2:width]
        if compact:
            own = own[:, 0:width // 4] + own[:, width // 4:width // 2]
        parts.append(own)
        power = power * offset
    if compact:
        scal = jnp.concatenate(parts + parts, axis=1)
        side = lax.broadcasted_iota(jnp.int32, (1, lanes), 1) >= width
        keep = jnp.where(flip, side.astype(f32), 1.0 - side.astype(f32)) > 0.5
        for r in range(rows_owned):
            six = packs[r]
            row = six[0:1]
            for f in range(1, feeds):
                row = jnp.where(feed == f, six[f:f + 1], row)
            half_row = jnp.where(feed >= 2, six[5:6], six[4:5])
            image_ref[r, CELLS:CELLS + 2, :] = jnp.concatenate(
                [row, jnp.where(keep, half_row, scal)], axis=0
            )
    else:
        scal = jnp.concatenate(parts, axis=1)
        fill = jnp.zeros((8 - share - 1, lanes), f32)
    for r in range(0 if compact else rows_owned):
        quarter = packs[r][0:share]
        for f in range(1, feeds):
            quarter = jnp.where(feed == f, packs[r][f * share:(f + 1) * share], quarter)
        image_ref[r, CELLS:CELLS + 8, :] = jnp.concatenate([quarter, scal, fill], axis=0)

    def scatter(d):
        for e in range(4):
            r = jnp.maximum(index_ref[d + e], 0)
            pay_ref[pl.ds((d + e) * rows_out, rows_out), :] = image_ref[r, 0:rows_out, :]

    each(scatter)


def final_kernel(
    recv_ref, prior_ref, sums_ref, w_ref, maps_ref,
    x_out, r_out, sky_out,
    y0_ref, y1_ref, y2_ref, x_ref, r_ref, sky_ref, sems,
    *, slots, feeds, samples, share, rows_in, compact,
):
    lanes = recv_ref.shape[1]
    sources = recv_ref.shape[0] // rows_in
    width = lanes // 2
    nb = lanes // CELLS
    prior = prior_ref[...]
    mean = shift_of(prior)
    offset = prior - mean
    sigma = mean + float(samples)
    sides = [None, None]
    for d in range(sources):
        at = d * rows_in + CELLS + share
        side = d // slots % 2 if compact else 0
        now = recv_ref[at:at + 1, :]
        sides[side] = now if sides[side] is None else sides[side] + now
    scal = sides[0][:, width:lanes] + sides[1][:, 0:width] if compact else sides[0]
    quarter = scal.shape[1] // 4
    rr0, rz, zz, zw = [
        jnp.sum(scal[:, i * quarter:(i + 1) * quarter], axis=1, keepdims=True) for i in range(4)
    ]
    gamma = rz / rr0
    alpha0 = 1.0 / (sigma + gamma)
    ee = zz - gamma * rz
    rr1 = alpha0 * alpha0 * ee
    beta = rr1 / rr0
    e_a_e = sigma * ee + (zw - 2.0 * gamma * zz + gamma * gamma * rz)
    alpha1 = rr1 / (alpha0 * alpha0 * e_a_e - rr1 * beta / alpha0)
    lead = alpha0 * gamma + beta
    slack = 1.0 - alpha1 * sigma
    x_r = alpha0 + alpha1 * lead
    x_z = -alpha0 * alpha1
    r_r = alpha0 * gamma * slack - alpha1 * sigma * beta
    r_z = -alpha0 * slack - alpha1 * lead
    r_w = alpha0 * alpha1
    packs = []
    for k in range(slots):
        base = [(f * slots + k) * rows_in for f in range(feeds)]
        pieces = [recv_ref[b + CELLS:b + CELLS + share, :] for b in base]
        if compact:
            ends = [recv_ref[b + CELLS + 1:b + CELLS + 2, :] for b in base]
            pieces += [pair_up(ends[0], ends[1]), pair_up(ends[2], ends[3])]
        packs.append(jnp.concatenate(pieces, axis=0))
        q0 = k * CELLS
        for f in range(0, feeds, 2):
            low = recv_ref[base[f]:base[f] + CELLS, :]
            high = recv_ref[base[f + 1]:base[f + 1] + CELLS, :]
            y0_ref[q0:q0 + CELLS, f * width:(f + 2) * width] = pair_up(low, high)
            y1_ref[q0:q0 + CELLS, f * width:(f + 2) * width] = turn(pair_up(high, low), width)
    y0 = y0_ref[...]
    y1 = y1_ref[...]
    sums = sums_ref[...]
    w = w_ref[...]
    lead_x = x_r + x_z * offset
    x_ref[...] = lead_x * sums - counted(w, lead_x * y0 + x_z * y1)
    sky_ref[...] = maps_ref[0] - x_r * maps_ref[1] - x_z * maps_ref[2]
    outs = [
        pltpu.make_async_copy(x_ref, x_out, sems.at[0]),
        pltpu.make_async_copy(sky_ref, sky_out, sems.at[1]),
        pltpu.make_async_copy(r_ref, r_out, sems.at[2]),
    ]
    outs[0].start()
    outs[1].start()
    for g, block in enumerate(gram_blocks(packs, compact)):
        stack = stacked(block)
        hits = jnp.sum(block, axis=1, keepdims=True) / float(samples)
        inverse = 1.0 / jnp.maximum(hits, 1.0)
        q0 = g * nb * CELLS
        part = y1_ref[q0:q0 + nb * CELLS, :]
        y2_ref[q0:q0 + nb * CELLS, :] = offset * part - inverse * gram_times(stack, part)
    second = r_z + r_w * offset
    lead_r = r_r + second * offset
    r_ref[...] = lead_r * sums - counted(w, lead_r * y0 + second * y1 + r_w * y2_ref[...])
    outs[2].start()
    for out in outs:
        out.wait()


def local(tod, pixels, block_slots, tile_lists, tile_place, prior):
    axes = ("feed", "tm")
    feeds = lax.axis_size("feed")
    owners = lax.axis_size("tm")
    slots = tile_lists.shape[1] * tile_lists.shape[2]
    assert slots == owners and feeds % 4 == 0
    rows_owned = tile_place.shape[0] // owners
    blocks, samples, channels = tod.shape
    cells = slots * CELLS
    width = channels // feeds
    lanes = 2 * width
    compact = lanes == 128 and feeds == 4
    gram_rows = 6 if compact else CELLS * CELLS // lanes
    rows = CELLS + gram_rows
    devices = feeds * owners
    chunk = max(n for n in range(1, 11) if samples % n == 0)
    small = devices * rows * lanes <= 1 << 18
    held = pltpu.VMEM if small else jax.ShapeDtypeStruct
    accs = []
    if blocks == cells == channels == 256 and chunk > 1:
        accs = [pltpu.ACC(n)((cells, channels), f32) for n in (0, 1, 0, 1, 1)]
    smem = pl.BlockSpec(memory_space=pltpu.SMEM)
    vmem = pl.BlockSpec(memory_space=pltpu.VMEM)

    hbm = pl.BlockSpec(memory_space=pl.ANY)
    payload, sums, counts, prior_row = pl.pallas_call(
        lambda *refs: pl.run_scoped(
            functools.partial(
                bin_kernel, *refs, slots=slots, feeds=feeds, rows_owned=rows_owned, chunk=chunk,
                compact=compact,
            ),
            *accs,
        ),
        in_specs=[smem, smem, vmem, vmem, hbm, hbm],
        out_specs=[vmem, vmem, vmem, vmem],
        out_shape=[
            held((devices * rows, lanes), f32),
            held((blocks, channels), f32),
            held((cells, blocks), bf16),
            held((1, channels), f32),
        ],
        scratch_shapes=[
            pltpu.VMEM((samples, blocks, channels), bf16),
            pltpu.VMEM((cells, channels), f32),
            pltpu.VMEM((cells, channels), f32),
            pltpu.VMEM((cells, lanes), f32),
            pltpu.SemaphoreType.DMA,
            pltpu.SemaphoreType.DMA((samples // chunk,)),
        ],
        name="bin_samples",
    )(
        tile_lists.reshape(slots),
        tile_place,
        block_slots.reshape(1, blocks),
        pixels.T,
        prior.reshape(1, channels),
        tod.transpose(1, 0, 2),
    )
    received = lax.all_to_all(
        payload.reshape(devices, 1, rows * lanes), axes, split_axis=0, concat_axis=0, tiled=True
    ).reshape(devices * rows, lanes)
    owned_cells = rows_owned * CELLS
    share = 1 if compact else gram_rows // feeds
    rows_back = CELLS + share + 1
    if not compact:
        rows_back = -(-rows_back // 8) * 8
    answer, maps, weights = pl.pallas_call(
        lambda *refs: owner_kernel(
            *refs, feeds=feeds, rows_owned=rows_owned, samples=samples, rows=rows,
            rows_out=rows_back, compact=compact
        ),
        in_specs=[vmem, vmem, vmem, vmem],
        out_specs=[vmem, vmem, vmem],
        out_shape=[
            held((devices * rows_back, lanes), f32),
            held((3, owned_cells, width), f32),
            held((blocks, cells), bf16),
        ],
        scratch_shapes=[
            pltpu.SMEM((devices,), jnp.int32),
            *[pltpu.VMEM((rows_owned, rows, lanes), f32) for _ in range(4)],
            pltpu.VMEM((rows_owned, CELLS + 8, lanes), f32),
        ],
        name="solve_tiles",
    )(near(received, small), near(prior_row, small), near(sums, small), near(counts, small))
    returned = lax.all_to_all(
        answer.reshape(devices, 1, rows_back * lanes), axes, split_axis=0, concat_axis=0, tiled=True
    ).reshape(devices * rows_back, lanes)
    drift, leftover, sky = pl.pallas_call(
        lambda *refs: final_kernel(
            *refs, slots=slots, feeds=feeds, samples=samples, share=share, rows_in=rows_back,
            compact=compact,
        ),
        in_specs=[vmem, vmem, vmem, vmem, vmem],
        out_specs=[hbm, hbm, hbm],
        out_shape=[
            jax.ShapeDtypeStruct((blocks, channels), f32),
            jax.ShapeDtypeStruct((blocks, channels), f32),
            jax.ShapeDtypeStruct((owned_cells, width), f32),
        ],
        scratch_shapes=[
            pltpu.VMEM((cells, channels), f32),
            pltpu.VMEM((cells, channels), f32),
            pltpu.VMEM((cells, channels), f32),
            pltpu.VMEM((blocks, channels), f32),
            pltpu.VMEM((blocks, channels), f32),
            pltpu.VMEM((owned_cells, width), f32),
            pltpu.SemaphoreType.DMA((3,)),
        ],
        name="finish",
    )(near(returned, small), near(prior_row, small), near(sums, small), near(weights, small), near(maps, small))
    return drift, leftover, sky.reshape(rows_owned, CELLS, width)


def solution(mesh):
    return jax.shard_map(
        local,
        mesh=mesh,
        in_specs=(
            P(("feed", "tm"), None, None),
            P(("feed", "tm"), None),
            P(("feed", "tm")),
            P(("feed", "tm"), None, None),
            P(),
            P(),
        ),
        out_specs=(P(("feed", "tm"), None), P(("feed", "tm"), None), P("tm", None, "feed")),
        check_vma=False,
    )
```
